32 devices in a mesh: section: 2 (over core), block: 16 (over z, y, x).
Axes of the slice: x: 2, y: 2, z: 4, core: 2. Of those that a mesh axis runs over, the one named last changes fastest.
Arguments:
- state: float32 [2, 16, 5, 32, 1024], P('section', 'block'), may hold values from -1 to 3.5, as said below
- mean_flow: float32 [16, 5, 32, 1024], P('block'), may hold values from -0.5 to 1.5, as said below
- les_owner: int32 [16], replicated, may hold values from 0 to 15, each once
- ac_owner: int32 [16], replicated, may hold values from 0 to 15, each once
- les_nbr: int32 [16, 6], replicated, may hold values from -1 to 15, as said below
- ac_nbr: int32 [16, 6], replicated, may hold values from -1 to 15, as said below
- coupling: int32 [16], replicated, may hold values from 0 to 15, each once
Outputs:
- advanced: float32 [2, 16, 5, 32, 1024], P('section', 'block')
The draws below stay inside these ranges and needn't reach their ends.
Inputs may be any that keep to these rules, and one draw needn't show every extreme that they name: `state`: section 0: density 1 to 1.5, momenta -0.4 to 0.4, pressure 0.4 (E - m.m / (2 r)) 0.7 to 1.3. Section 1: all entries -1 to 1. `mean_flow`: mean density 0.8 to 1.5, mean velocities -0.5 to 0.5, mean pressure 0.7 to 1.3. `les_nbr`: blocks sit on a 4 x 4 x 16/16 grid of equal blocks; an entry names the block beside it across that face, and that block names it back across the opposite face. `ac_nbr`: blocks sit on a 4 x 4 x 16/16 grid of equal blocks; an entry names the block beside it across that face, and that block names it back across the opposite face.
All inputs are finite; a program needn't handle non-finite values.
Results may differ from the reference program's by a relative error of at most 0.0003.
Values may be sent and summed in bfloat16 or wider, within the bound.
No kernel may reach another device: no remote copies, remote signals or barrier semaphores. Data moves between devices by JAX's collectives and lax.ppermute only.
A program may use at most 128 MiB of HBM per device.

```python
import jax
import jax.numpy as jnp
from jax import lax

BS = 32
STEPS = 2
NBLK = 16


def grid_neighbours(key):
    layers_z = NBLK // 16
    position = jax.random.permutation(key, NBLK).astype(jnp.int32)
    coord_x = position // (4 * layers_z)
    coord_y = position // layers_z % 4
    coord_z = position % layers_z
    block_at = jnp.argsort(position).astype(jnp.int32)
    offsets = [(-1, 0, 0), (1, 0, 0), (0, -1, 0), (0, 1, 0), (0, 0, -1), (0, 0, 1)]
    columns = []
    for step_x, step_y, step_z in offsets:
        next_x = coord_x + step_x
        next_y = coord_y + step_y
        next_z = coord_z + step_z
        inside = (next_x >= 0) & (next_x < 4) & (next_y >= 0) & (next_y < 4) & (next_z >= 0) & (next_z < layers_z)
        target = jnp.clip(next_x * 4 * layers_z + next_y * layers_z + next_z, 0, NBLK - 1)
        columns.append(jnp.where(inside, block_at[target], -1))
    return jnp.stack(columns, axis=1).astype(jnp.int32)


def draw_les_nbr(key, part):
    return grid_neighbours(jax.random.fold_in(key, 11))


def draw_ac_nbr(key, part):
    return grid_neighbours(jax.random.fold_in(key, 23))


def draw_state(key, part):
    keys = jax.random.split(jax.random.fold_in(key, 37), 2)
    shape_one = (NBLK, BS, BS * BS)
    uniform_part = jax.random.uniform(keys[0], (5,) + shape_one, jnp.float32)
    density = 1.0 + 0.5 * uniform_part[0]
    momentum = -0.4 + 0.8 * uniform_part[1:4]
    pressure = 0.7 + 0.6 * uniform_part[4]
    energy = pressure / 0.4 + 0.5 * jnp.sum(momentum * momentum, axis=0) / density
    les_part = jnp.concatenate([density[None], momentum, energy[None]], axis=0)
    acoustic = jax.random.uniform(keys[1], (5,) + shape_one, jnp.float32, -1.0, 1.0)
    stacked = jnp.stack([les_part, acoustic])
    return jnp.transpose(stacked, (0, 2, 1, 3, 4)).astype(jnp.float32)


def draw_mean_flow(key, part):
    uniform_part = jax.random.uniform(jax.random.fold_in(key, 41), (5, NBLK, BS, BS * BS), jnp.float32)
    density = 0.8 + 0.7 * uniform_part[0]
    velocity = -0.5 + uniform_part[1:4]
    pressure = 0.7 + 0.6 * uniform_part[4]
    stacked = jnp.concatenate([density[None], velocity, pressure[None]], axis=0)
    return jnp.transpose(stacked, (1, 0, 2, 3)).astype(jnp.float32)


def setup_inputs(seed: int = 0) -> dict:
    seeds = jax.random.split(jax.random.key(seed), 8)
    state = draw_state(jax.random.fold_in(seeds[7], 71), 0)
    mean_flow = draw_mean_flow(jax.random.fold_in(seeds[7], 71), 0)
    les_owner = jax.random.permutation(seeds[2], NBLK).astype(jnp.int32)
    ac_owner = jax.random.permutation(seeds[3], NBLK).astype(jnp.int32)
    les_nbr = draw_les_nbr(jax.random.fold_in(seeds[7], 71), 0)
    ac_nbr = draw_ac_nbr(jax.random.fold_in(seeds[7], 71), 0)
    coupling = jax.random.permutation(seeds[6], NBLK).astype(jnp.int32)
    return {"state": state, "mean_flow": mean_flow, "les_owner": les_owner, "ac_owner": ac_owner, "les_nbr": les_nbr, "ac_nbr": ac_nbr, "coupling": coupling}


GAMMA_LESS = 0.4
DT_LES = 0.2
DT_AC = 0.3
VISCOSITY = 0.05
FEEDBACK_GAIN = 0.5


def face_layers(volume):
    num_blocks, num_vars, cube_side, face_cells = volume.shape
    members = [
        volume[:, :, 0, :],
        volume[:, :, cube_side - 1, :],
        volume[:, :, :, 0:cube_side].reshape(num_blocks, num_vars, face_cells),
        volume[:, :, :, (cube_side - 1) * cube_side:].reshape(num_blocks, num_vars, face_cells),
        volume[:, :, :, 0::cube_side].reshape(num_blocks, num_vars, face_cells),
        volume[:, :, :, cube_side - 1::cube_side].reshape(num_blocks, num_vars, face_cells),
    ]
    return jnp.stack(members, axis=1)


def neighbours(volume, halo_cells):
    num_blocks, num_vars, cube_side, face_cells = volume.shape

    def face_grid(direction):
        return halo_cells[:, direction].reshape(num_blocks, num_vars, cube_side, cube_side)

    low_x = jnp.concatenate([halo_cells[:, 0][:, :, None, :], volume[:, :, :-1, :]], axis=2)
    high_x = jnp.concatenate([volume[:, :, 1:, :], halo_cells[:, 1][:, :, None, :]], axis=2)
    low_y = jnp.concatenate([face_grid(2), volume[:, :, :, :-cube_side]], axis=3)
    high_y = jnp.concatenate([volume[:, :, :, cube_side:], face_grid(3)], axis=3)
    z_index = lax.broadcasted_iota(jnp.int32, (1, 1, 1, face_cells), 3) % cube_side
    low_z = jnp.where(z_index == 0, jnp.repeat(face_grid(4), cube_side, axis=3), jnp.roll(volume, 1, axis=3))
    high_z = jnp.where(z_index == cube_side - 1, jnp.repeat(face_grid(5), cube_side, axis=3), jnp.roll(volume, -1, axis=3))
    return ((low_x, high_x), (low_y, high_y), (low_z, high_z))


def primitives(conserved):
    density = conserved[:, 0]
    momentum = conserved[:, 1:4]
    energy = conserved[:, 4]
    velocity = momentum / density[:, None]
    pressure = GAMMA_LESS * (energy - 0.5 * jnp.sum(momentum * velocity, axis=1))
    return momentum, energy, velocity, pressure


def flux_along(conserved, axis_k):
    momentum, energy, velocity, pressure = primitives(conserved)
    normal_speed = velocity[:, axis_k]
    members = [momentum[:, axis_k]]
    for component in range(3):
        entry_term = momentum[:, component] * normal_speed
        if component == axis_k:
            entry_term = entry_term + pressure
        members.append(entry_term)
    members.append((energy + pressure) * normal_speed)
    return jnp.stack(members, axis=1), velocity


def les_both(conserved, halo_cells):
    pairs = neighbours(conserved, halo_cells)
    momentum, energy, velocity, pressure = primitives(conserved)
    flux_sum = jnp.zeros_like(conserved)
    laplace = -6.0 * conserved
    gradient = []
    for axis_k in range(3):
        low_side, high_side = pairs[axis_k]
        flux_low, speed_low = flux_along(low_side, axis_k)
        flux_high, speed_high = flux_along(high_side, axis_k)
        flux_sum = flux_sum + 0.5 * (flux_high - flux_low)
        laplace = laplace + low_side + high_side
        gradient.append(0.5 * (speed_high - speed_low))
    vort_x = gradient[1][:, 2] - gradient[2][:, 1]
    vort_y = gradient[2][:, 0] - gradient[0][:, 2]
    vort_z = gradient[0][:, 1] - gradient[1][:, 0]
    lamb_vector = jnp.stack([
        vort_y * velocity[:, 2] - vort_z * velocity[:, 1],
        vort_z * velocity[:, 0] - vort_x * velocity[:, 2],
        vort_x * velocity[:, 1] - vort_y * velocity[:, 0],
    ], axis=1).astype(jnp.bfloat16)
    updated = conserved + DT_LES * (VISCOSITY * laplace - flux_sum)
    return updated, lamb_vector


def acoustic_advance(perturb, halo_cells, mean_state, source):
    pairs = neighbours(perturb, halo_cells)
    slopes = [0.5 * (high_side - low_side) for low_side, high_side in pairs]
    mean_density = mean_state[:, 0]
    mean_pressure = mean_state[:, 4]
    carried = mean_state[:, 1][:, None] * slopes[0] + mean_state[:, 2][:, None] * slopes[1] + mean_state[:, 3][:, None] * slopes[2]
    divergence = slopes[0][:, 1] + slopes[1][:, 2] + slopes[2][:, 3]
    members = [carried[:, 0] + mean_density * divergence]
    for axis_k in range(3):
        members.append(carried[:, 1 + axis_k] + slopes[axis_k][:, 4] / mean_density + source[:, axis_k])
    members.append(carried[:, 4] + 1.4 * mean_pressure * divergence)
    return perturb - DT_AC * jnp.stack(members, axis=1)


def invert_list(owner_list):
    count = owner_list.shape[0]
    return jnp.zeros((count,), jnp.int32).at[owner_list].set(jnp.arange(count, dtype=jnp.int32))


def halo_of(values, owner_list, partner_table):
    inverse = invert_list(owner_list)
    face_cells = face_layers(values)
    partner = partner_table[inverse]
    present = partner >= 0
    source_slot = owner_list[jnp.maximum(partner, 0)]
    opposite = jnp.array([1, 0, 3, 2, 5, 4], jnp.int32)
    picked = face_cells[source_slot, opposite[None, :]]
    return jnp.where(present[:, :, None, None], picked, face_cells)


def les_single(items):
    updated, lamb_vector = les_both(items[0][None], items[1][None])
    return updated[0], lamb_vector[0]


def acoustic_single(items):
    return acoustic_advance(items[0][None], items[1][None], items[2][None], items[3][None].astype(jnp.float32))[0]


def reference(state, mean_flow, les_owner, ac_owner, les_nbr, ac_nbr, coupling):
    inverse_ac = invert_list(ac_owner)
    coupled = les_owner[coupling[inverse_ac]]
    feed_slot = ac_owner[invert_list(coupling)[invert_list(les_owner)]]
    les_values = state[0]
    ac_values = state[1]
    for step_index in range(STEPS):
        les_halo = halo_of(les_values, les_owner, les_nbr)
        ac_halo = halo_of(ac_values, ac_owner, ac_nbr)
        back = ac_values[:, 1:4].astype(jnp.bfloat16)
        les_next, lamb_vector = lax.map(les_single, (les_values, les_halo))
        source = lamb_vector[coupled]
        feedback = back[feed_slot].astype(jnp.float32)
        ac_values = lax.map(acoustic_single, (ac_values, ac_halo, mean_flow, source))
        les_values = les_next.at[:, 1:4].add(DT_LES * FEEDBACK_GAIN * feedback)
    return jnp.stack([les_values, ac_values])
```

```python
import functools

import jax
import jax.numpy as jnp
from jax import lax
from jax.experimental import pallas as pl
from jax.experimental.pallas import tpu as pltpu
from jax.sharding import PartitionSpec as P


STEPS = 2

GAMMA_LESS = 0.4
DT_LES = 0.2
DT_AC = 0.3
VISCOSITY = 0.05
FEEDBACK_GAIN = 0.5

WIRE = jnp.int16
SCALE_IN = 32000.0
SCALE_MID = 8192.0
SCALE_OUT = 4096.0
OFFSETS = ((1.25, 0.0, 0.0, 0.0, 2.6), (0.0, 0.0, 0.0, 0.0, 0.0))
MEAN_OFFSETS = (1.0, 0.0, 0.0, 0.0, 1.0)
PAIRS = ((0, 1), (2, 3), (4, 4))

LANES = 128
FACES = 6
COLUMNS = FACES + 1


class Plan:
    def __init__(self, blocks, sections, num_vars, side):
        self.blocks = blocks
        self.devices = blocks * sections
        self.vars = num_vars
        self.side = side
        self.layers_z = blocks // 16
        self.ny = side * side // LANES
        self.nx = self.devices // self.ny
        self.xs = side // self.nx
        self.half = self.xs // sections
        self.core_rows = num_vars * self.xs
        self.y_base = self.core_rows
        self.mean_base = self.y_base + len(PAIRS) * self.xs
        self.x_base = self.mean_base + num_vars * self.half
        self.rows = -(-(self.x_base + 2 * num_vars) // 16) * 16
        assert sections == 2 and LANES == 4 * side and 2 * self.half * self.nx == side

    def piece(self, device):
        section, block = device // self.blocks, device % self.blocks
        low, mid, high = block % 2, block // 2 % 2, block // 4
        ring = section if low == 0 else 3 - section
        depth = high % 4
        return ring + 4 * (high // 4), depth if mid == 0 else 7 - depth

    def own_piece(self, section, block):
        low, mid, high = block % 2, block // 2 % 2, block // 4
        ring = jnp.where(low == 0, section, 3 - section)
        depth = high % 4
        return ring + 4 * (high // 4), jnp.where(mid == 0, depth, 7 - depth)

    def permutation(self, step_x, step_y):
        at = {self.piece(d): d for d in range(self.devices)}
        assert len(at) == self.devices
        pairs = []
        for device in range(self.devices):
            px, py = self.piece(device)
            pairs.append((device, at[((px + step_x) % self.nx, (py + step_y) % self.ny)]))
        return pairs


def to_wire(scaled):
    return lax.round(scaled, lax.RoundingMethod.TO_NEAREST_EVEN).astype(jnp.int32).astype(WIRE)


def from_wire(sent):
    return sent.astype(jnp.int32).astype(jnp.float32)


def roll_lanes(tile, shift):
    return pltpu.roll(tile, shift % LANES, 1)


def roll_rows(tile, shift):
    rows = tile.shape[0]
    shift = shift % rows
    if rows % 8 == 0:
        return pltpu.roll(tile, shift, 0)
    return jnp.concatenate([tile[rows - shift :], tile[: rows - shift]], axis=0)


def lane_index(rows):
    return lax.broadcasted_iota(jnp.int32, (rows, LANES), 1)


def pack_kernel(
    plan, state, mean, les_owner, ac_owner, les_nbr, ac_nbr, coupling,
    message, table, raw, filled, les_inv, ac_inv, pair_inv,
):
    section = lax.axis_index("section")
    px, py = plan.own_piece(section, lax.axis_index("block"))
    xs, side, half = plan.xs, plan.side, plan.half
    width = side * side
    for v in range(plan.vars):
        offset = jnp.where(section == 0, OFFSETS[0][v], OFFSETS[1][v])
        raw[v] = (state[v] - offset) * SCALE_IN
    lane = lane_index(xs)
    for device in range(plan.devices):
        tx, ty = plan.piece(device)
        x0, l0 = tx * xs, ty * LANES
        here = slice(l0, l0 + LANES)
        before = (l0 - LANES) % width
        after = (l0 + LANES) % width
        for v in range(plan.vars):
            filled[device, v * xs : (v + 1) * xs, :] = raw[v, x0 : x0 + xs, here]
            filled[device, plan.x_base + v, :] = raw[v, (x0 - 1) % side, here]
            filled[device, plan.x_base + plan.vars + v, :] = raw[v, (x0 + xs) % side, here]
            first, second = mean[v, x0 : x0 + half, here], mean[v, x0 + half : x0 + xs, here]
            piece = jnp.where(section == 0, first, second)
            base = plan.mean_base + v * half
            filled[device, base : base + half, :] = (piece - MEAN_OFFSETS[v]) * SCALE_IN
        for i, (a, b) in enumerate(PAIRS):
            low_a = raw[a, x0 : x0 + xs, before : before + LANES]
            low_b = raw[b, x0 : x0 + xs, before : before + LANES]
            high_a = raw[a, x0 : x0 + xs, after : after + LANES]
            high_b = raw[b, x0 : x0 + xs, after : after + LANES]
            low = jnp.where(lane < side, roll_lanes(low_a, side), roll_lanes(high_b, side))
            high = jnp.where(lane < 3 * side, roll_lanes(low_b, -side), roll_lanes(high_a, -side))
            base = plan.y_base + i * xs
            filled[device, base : base + xs, :] = jnp.where(lane < 2 * side, low, high)
        used = plan.x_base + 2 * plan.vars
        if used < plan.rows:
            filled[device, used:, :] = jnp.zeros((plan.rows - used, LANES), jnp.float32)
        message[device] = to_wire(filled[device])

    def invert(i, carry):
        les_inv[les_owner[i]] = i
        ac_inv[ac_owner[i]] = i
        pair_inv[coupling[i]] = i
        return carry

    lax.fori_loop(0, plan.blocks, invert, 0)
    at_edge = (px == 0, px == plan.nx - 1, py == 0, py == plan.ny - 1, True, True)

    def look_up(slot, carry):
        les_block = les_inv[slot]
        ac_block = ac_inv[slot]
        for kind, (block, nbr, owner) in enumerate(
            ((les_block, les_nbr, les_owner), (ac_block, ac_nbr, ac_owner))
        ):
            for face in range(FACES):
                other = nbr[block, face]
                source = jnp.where(other < 0, -1, owner[jnp.maximum(other, 0)])
                if face < 4:
                    source = jnp.where(at_edge[face], source, slot)
                table[(kind * COLUMNS + face) * plan.blocks + slot] = source
        table[FACES * plan.blocks + slot] = ac_owner[pair_inv[les_block]]
        table[(COLUMNS + FACES) * plan.blocks + slot] = les_owner[coupling[ac_block]]
        return carry

    lax.fori_loop(0, plan.blocks, look_up, 0)


def sides(plan, table, kind, slot, core, x_halo, y_halo):
    xs, side = plan.xs, plan.side
    lane = lane_index(xs)
    row = lax.broadcasted_iota(jnp.int32, (xs, LANES), 0)
    depth = lane % side
    found = [table[(kind * COLUMNS + face) * plan.blocks + slot] for face in range(FACES)]
    inside = [f >= 0 for f in found]
    found = [jnp.maximum(f, 0) for f in found]
    own = [core(kind, slot, v) for v in range(plan.vars)]
    shifted = [[] for _ in range(FACES)]
    for v, tile in enumerate(own):
        low = jnp.where(inside[0], x_halo(kind, found[0], v, 0), tile[0:1])
        high = jnp.where(inside[1], x_halo(kind, found[1], v, 1), tile[xs - 1 : xs])
        shifted[0].append(jnp.where(row == 0, low, roll_rows(tile, 1)))
        shifted[1].append(jnp.where(row == xs - 1, high, roll_rows(tile, -1)))
        low = jnp.where(inside[2], y_halo(kind, found[2], v, 0), tile)
        high = jnp.where(inside[3], y_halo(kind, found[3], v, 1), tile)
        shifted[2].append(jnp.where(lane < side, low, roll_lanes(tile, side)))
        shifted[3].append(jnp.where(lane >= LANES - side, high, roll_lanes(tile, -side)))
        low, high = tile, tile
        if plan.layers_z > 1:
            low = jnp.where(inside[4], roll_lanes(core(kind, found[4], v), 1 - side), tile)
            high = jnp.where(inside[5], roll_lanes(core(kind, found[5], v), side - 1), tile)
        shifted[4].append(jnp.where(depth == 0, low, roll_lanes(tile, 1)))
        shifted[5].append(jnp.where(depth == side - 1, high, roll_lanes(tile, -1)))
    return own, shifted


def primitives(conserved):
    density, energy = conserved[0], conserved[4]
    momentum = conserved[1:4]
    inverse = 1.0 / density
    velocity = [m * inverse for m in momentum]
    kinetic = momentum[0] * velocity[0] + momentum[1] * velocity[1] + momentum[2] * velocity[2]
    return momentum, energy, velocity, GAMMA_LESS * (energy - 0.5 * kinetic)


def flux_along(conserved, axis):
    momentum, energy, velocity, pressure = primitives(conserved)
    normal = velocity[axis]
    flux = [momentum[axis]]
    for component in range(3):
        entry = momentum[component] * normal
        flux.append(entry + pressure if component == axis else entry)
    flux.append((energy + pressure) * normal)
    return flux, velocity


def cross(a, b):
    return [
        a[1] * b[2] - a[2] * b[1],
        a[2] * b[0] - a[0] * b[2],
        a[0] * b[1] - a[1] * b[0],
    ]


def as_bf16(tile):
    return tile.astype(jnp.bfloat16).astype(jnp.float32)


def les_slot(plan, own, shifted):
    count = plan.vars
    total = [(1.0 - 6.0 * DT_LES * VISCOSITY) * own[v] for v in range(count)]
    gradient = []
    for axis in range(3):
        low, high = shifted[2 * axis], shifted[2 * axis + 1]
        flux_low, speed_low = flux_along(low, axis)
        flux_high, speed_high = flux_along(high, axis)
        for v in range(count):
            total[v] = total[v] + (
                DT_LES * VISCOSITY * (low[v] + high[v]) - 0.5 * DT_LES * (flux_high[v] - flux_low[v])
            )
        gradient.append([0.5 * (h - w) for h, w in zip(speed_high, speed_low)])
    velocity = [m * (1.0 / own[0]) for m in own[1:4]]
    vorticity = [
        gradient[1][2] - gradient[2][1],
        gradient[2][0] - gradient[0][2],
        gradient[0][1] - gradient[1][0],
    ]
    return total, [as_bf16(t) for t in cross(vorticity, velocity)]


def ac_slot(plan, own, shifted, mean, source):
    slope = [
        [0.5 * (h - w) for h, w in zip(shifted[2 * axis + 1], shifted[2 * axis])] for axis in range(3)
    ]
    carried = [
        mean[1] * slope[0][v] + mean[2] * slope[1][v] + mean[3] * slope[2][v]
        for v in range(plan.vars)
    ]
    divergence = slope[0][1] + slope[1][2] + slope[2][3]
    inverse = 1.0 / mean[0]
    change = [carried[0] + mean[0] * divergence]
    for axis in range(3):
        change.append(carried[1 + axis] + slope[axis][4] * inverse + source[axis])
    change.append(carried[4] + 1.4 * mean[4] * divergence)
    return [g - DT_AC * c for g, c in zip(own, change)]


def advance(plan, table, core, x_halo, y_halo, mean, lamb, store):
    xs = plan.xs

    def les_body(slot, carry):
        own, shifted = sides(plan, table, 0, slot, core, x_halo, y_halo)
        total, vector = les_slot(plan, own, shifted)
        partner = table[FACES * plan.blocks + slot]
        for j in range(3):
            back = as_bf16(core(1, partner, 1 + j))
            total[1 + j] = total[1 + j] + DT_LES * FEEDBACK_GAIN * back
            lamb[slot, j * xs : (j + 1) * xs, :] = vector[j]
        store(0, slot, total)
        return carry

    def ac_body(slot, carry):
        own, shifted = sides(plan, table, 1, slot, core, x_halo, y_halo)
        partner = table[(COLUMNS + FACES) * plan.blocks + slot]
        source = [lamb[partner, j * xs : (j + 1) * xs, :] for j in range(3)]
        store(1, slot, ac_slot(plan, own, shifted, mean(slot), source))
        return carry

    lax.fori_loop(0, plan.blocks, les_body, 0, unroll=2)
    lax.fori_loop(0, plan.blocks, ac_body, 0, unroll=2)


def tile_rows(plan, v):
    return slice(v * plan.xs, (v + 1) * plan.xs)


def first_kernel(
    plan, table, message,
    after, mean_out, x_up, x_down, y_up, y_down,
    arrived, lamb, x_up_raw, x_down_raw, y_up_raw, y_down_raw,
):
    xs, side, count, blocks, half = plan.xs, plan.side, plan.vars, plan.blocks, plan.half
    lane = lane_index(xs)

    def read(m, carry):
        arrived[m] = from_wire(message[m]) * (1.0 / SCALE_IN)
        return carry

    lax.fori_loop(0, plan.devices, read, 0, unroll=2)

    def read_mean(slot, carry):
        for v in range(count):
            base = plan.mean_base + v * half
            for part in range(plan.devices // blocks):
                rows = arrived[part * blocks + slot, base : base + half, :]
                start = v * xs + part * half
                mean_out[slot, start : start + half, :] = rows + MEAN_OFFSETS[v]
        return carry

    lax.fori_loop(0, blocks, read_mean, 0)

    def shift_back(tile, kind, v):
        return tile if OFFSETS[kind][v] == 0.0 else tile + OFFSETS[kind][v]

    def core(kind, slot, v):
        return shift_back(arrived[kind * blocks + slot, tile_rows(plan, v), :], kind, v)

    def x_halo(kind, slot, v, end):
        at = plan.x_base + end * count + v
        return shift_back(arrived[kind * blocks + slot, at : at + 1, :], kind, v)

    def y_halo(kind, slot, v, end):
        base = plan.y_base + (v // 2) * xs
        tile = arrived[kind * blocks + slot, base : base + xs, :]
        if v % 2 == 1:
            tile = roll_lanes(tile, 2 * side)
        return shift_back(tile, kind, v)

    def mean(slot):
        return [mean_out[slot, tile_rows(plan, v), :] for v in range(count)]

    def store(kind, slot, tiles):
        m = kind * blocks + slot
        quarter = m % 4
        rest = plan.devices * xs + (m // 4) * xs
        up = down = None
        for v, tile in enumerate(tiles):
            after[m, tile_rows(plan, v), :] = tile
            coded = (tile - OFFSETS[kind][v]) * SCALE_MID
            x_up_raw[pl.ds(m * count + v, 1), :] = coded[xs - 1 : xs]
            x_down_raw[pl.ds(m * count + v, 1), :] = coded[0:1]
            if v < 4:
                high = roll_lanes(coded, side * (v + 1))
                low = roll_lanes(coded, side * v)
                mine = lane >= side * v
                up = high if v == 0 else jnp.where(mine, high, up)
                down = low if v == 0 else jnp.where(mine, low, down)
            else:
                high = pltpu.roll(coded, (side * (quarter + 1)) % LANES, 1)
                low = pltpu.roll(coded, side * quarter, 1)
                mine = lane >= side * quarter
                where = pl.ds(pl.multiple_of(rest, xs), xs)
                y_up_raw[where, :] = jnp.where(mine, high, y_up_raw[where, :])
                y_down_raw[where, :] = jnp.where(mine, low, y_down_raw[where, :])
        where = pl.ds(pl.multiple_of(m * xs, xs), xs)
        y_up_raw[where, :] = up
        y_down_raw[where, :] = down

    advance(plan, table, core, x_halo, y_halo, mean, lamb, store)
    for raw, out in (
        (x_up_raw, x_up), (x_down_raw, x_down), (y_up_raw, y_up), (y_down_raw, y_down),
    ):
        out[...] = to_wire(raw[...])


def last_kernel(
    plan, table, before, mean_in, x_low, x_high, y_low, y_high,
    message, lamb, x_low_raw, x_high_raw, y_low_raw, y_high_raw, coded,
):
    xs, side, count, blocks = plan.xs, plan.side, plan.vars, plan.blocks
    for raw, sent in (
        (x_low_raw, x_low), (x_high_raw, x_high), (y_low_raw, y_low), (y_high_raw, y_high),
    ):
        raw[...] = from_wire(sent[...]) * (1.0 / SCALE_MID)

    def shift_back(tile, kind, v):
        return tile if OFFSETS[kind][v] == 0.0 else tile + OFFSETS[kind][v]

    def core(kind, slot, v):
        return before[kind * blocks + slot, tile_rows(plan, v), :]

    def x_halo(kind, slot, v, end):
        raw = x_high_raw if end else x_low_raw
        return shift_back(raw[pl.ds((kind * blocks + slot) * count + v, 1), :], kind, v)

    def y_halo(kind, slot, v, end):
        raw = y_high_raw if end else y_low_raw
        m = kind * blocks + slot
        target = 3 * side if end else 0
        if v < 4:
            tile = raw[pl.ds(pl.multiple_of(m * xs, xs), xs), :]
            tile = roll_lanes(tile, target - side * v)
        else:
            rest = plan.devices * xs + (m // 4) * xs
            tile = raw[pl.ds(pl.multiple_of(rest, xs), xs), :]
            tile = pltpu.roll(tile, (target + LANES - side * (m % 4)) % LANES, 1)
        return shift_back(tile, kind, v)

    def mean(slot):
        return [mean_in[slot, tile_rows(plan, v), :] for v in range(count)]

    def store(kind, slot, tiles):
        for v, tile in enumerate(tiles):
            coded[kind * blocks + slot, tile_rows(plan, v), :] = (tile - OFFSETS[kind][v]) * SCALE_OUT

    advance(plan, table, core, x_halo, y_halo, mean, lamb, store)

    def write(m, carry):
        message[m] = to_wire(coded[m])
        return carry

    lax.fori_loop(0, plan.devices, write, 0, unroll=2)


def unpack_kernel(plan, message, out):
    section = lax.axis_index("section")
    xs = plan.xs
    for device in range(plan.devices):
        tx, ty = plan.piece(device)
        values = from_wire(message[device]) * (1.0 / SCALE_OUT)
        for v in range(plan.vars):
            offset = jnp.where(section == 0, OFFSETS[0][v], OFFSETS[1][v])
            out[v, tx * xs : (tx + 1) * xs, ty * LANES : (ty + 1) * LANES] = (
                values[v * xs : (v + 1) * xs] + offset
            )


def vmem(count):
    return [pl.BlockSpec(memory_space=pltpu.VMEM)] * count


def smem(count):
    return [pl.BlockSpec(memory_space=pltpu.SMEM)] * count


def on_device(plan, state, mean_flow, les_owner, ac_owner, les_nbr, ac_nbr, coupling):
    axes = ("section", "block")
    devices, blocks, count, xs = plan.devices, plan.blocks, plan.vars, plan.xs
    f32 = jnp.float32

    def array(dtype, *shape):
        return jax.ShapeDtypeStruct(shape, dtype)

    message, table = pl.pallas_call(
        functools.partial(pack_kernel, plan),
        out_shape=(
            array(WIRE, devices, plan.rows, LANES),
            array(jnp.int32, 2 * COLUMNS * blocks),
        ),
        in_specs=vmem(2) + smem(5),
        out_specs=tuple(vmem(1) + smem(1)),
        scratch_shapes=[
            pltpu.VMEM((count, plan.side, plan.side * plan.side), f32),
            pltpu.VMEM((devices, plan.rows, LANES), f32),
        ]
        + [pltpu.SMEM((blocks,), jnp.int32)] * 3,
        name="pack",
    )(state[0, 0], mean_flow[0], les_owner, ac_owner, les_nbr, ac_nbr, coupling)
    message = lax.all_to_all(message, axes, split_axis=0, concat_axis=0, tiled=True)

    x_rows = devices * count
    y_rows = devices * xs + devices // 4 * xs
    halo_shapes = [(x_rows, LANES)] * 2 + [(y_rows, LANES)] * 2
    halo_scratch = [pltpu.VMEM(shape, f32) for shape in halo_shapes]
    lamb_scratch = pltpu.VMEM((blocks, 3 * xs, LANES), f32)
    after, mean, *halos = pl.pallas_call(
        functools.partial(first_kernel, plan),
        out_shape=(
            array(f32, devices, plan.core_rows, LANES),
            array(f32, blocks, plan.core_rows, LANES),
            *(array(WIRE, *shape) for shape in halo_shapes),
        ),
        in_specs=smem(1) + vmem(1),
        out_specs=tuple(vmem(6)),
        scratch_shapes=[pltpu.VMEM((devices, plan.rows, LANES), f32), lamb_scratch] + halo_scratch,
        name="first_step",
    )(table, message)
    moves = [plan.permutation(*step) for step in ((1, 0), (-1, 0), (0, 1), (0, -1))]
    halos = [lax.ppermute(halo, axes, move) for halo, move in zip(halos, moves)]

    message = pl.pallas_call(
        functools.partial(last_kernel, plan),
        out_shape=array(WIRE, devices, plan.core_rows, LANES),
        in_specs=smem(1) + vmem(6),
        out_specs=vmem(1)[0],
        scratch_shapes=[lamb_scratch]
        + halo_scratch
        + [pltpu.VMEM((devices, plan.core_rows, LANES), f32)],
        name="last_step",
    )(table, after, mean, *halos)
    message = lax.all_to_all(message, axes, split_axis=0, concat_axis=0, tiled=True)

    result = pl.pallas_call(
        functools.partial(unpack_kernel, plan),
        out_shape=array(f32, *state.shape[2:]),
        in_specs=vmem(1),
        out_specs=vmem(1)[0],
        name="unpack",
    )(message)
    return result[None, None]


def solution(mesh):
    def program(state, mean_flow, les_owner, ac_owner, les_nbr, ac_nbr, coupling):
        plan = Plan(mesh.shape["block"], mesh.shape["section"], state.shape[2], state.shape[3])
        return jax.shard_map(
            functools.partial(on_device, plan),
            mesh=mesh,
            in_specs=(
                P("section", "block", None, None, None),
                P("block", None, None, None),
                P(),
                P(),
                P(),
                P(),
                P(),
            ),
            out_specs=P("section", "block", None, None, None),
            check_vma=False,
        )(state, mean_flow, les_owner, ac_owner, les_nbr, ac_nbr, coupling)

    return program
```

```python
import functools

import jax
import jax.numpy as jnp
from jax import lax
from jax.experimental import pallas as pl
from jax.experimental.pallas import tpu as pltpu
from jax.sharding import PartitionSpec as P


STEPS = 2

GAMMA_LESS = 0.4
DT_LES = 0.2
DT_AC = 0.3
VISCOSITY = 0.05
FEEDBACK_GAIN = 0.5

WIRE = jnp.int16
SCALE_IN = 32000.0
SCALE_MID = 8192.0
SCALE_OUT = 4096.0
OFFSETS = ((1.25, 0.0, 0.0, 0.0, 2.6), (0.0, 0.0, 0.0, 0.0, 0.0))
MEAN_OFFSETS = (1.0, 0.0, 0.0, 0.0, 1.0)
PAIRS = ((0, 1), (2, 3), (4, 4))

LANES = 128
FACES = 6
COLUMNS = FACES + 1


class Plan:
    def __init__(self, blocks, sections, num_vars, side):
        self.blocks = blocks
        self.devices = blocks * sections
        self.vars = num_vars
        self.side = side
        self.layers_z = blocks // 16
        self.ny = side * side // LANES
        self.nx = self.devices // self.ny
        self.xs = side // self.nx
        self.half = self.xs // sections
        self.core_rows = num_vars * self.xs
        self.y_base = self.core_rows
        self.mean_base = self.y_base + len(PAIRS) * self.xs
        self.x_base = self.mean_base + num_vars * self.half
        self.rows = -(-(self.x_base + 2 * num_vars) // 16) * 16
        assert sections == 2 and LANES == 4 * side and 2 * self.half * self.nx == side

    def piece(self, device):
        section, block = device // self.blocks, device % self.blocks
        low, mid, high = block % 2, block // 2 % 2, block // 4
        ring = section if low == 0 else 3 - section
        depth = high % 4
        return ring + 4 * (high // 4), depth if mid == 0 else 7 - depth

    def own_piece(self, section, block):
        low, mid, high = block % 2, block // 2 % 2, block // 4
        ring = jnp.where(low == 0, section, 3 - section)
        depth = high % 4
        return ring + 4 * (high // 4), jnp.where(mid == 0, depth, 7 - depth)

    def permutation(self, step_x, step_y):
        at = {self.piece(d): d for d in range(self.devices)}
        assert len(at) == self.devices
        pairs = []
        for device in range(self.devices):
            px, py = self.piece(device)
            pairs.append((device, at[((px + step_x) % self.nx, (py + step_y) % self.ny)]))
        return pairs


def to_wire(scaled):
    return lax.round(scaled, lax.RoundingMethod.TO_NEAREST_EVEN).astype(jnp.int32).astype(WIRE)


def from_wire(sent):
    return sent.astype(jnp.int32).astype(jnp.float32)


def roll_lanes(tile, shift):
    shift = shift % LANES
    return pltpu.roll(tile, shift, 1) if shift else tile


def roll_rows(tile, shift):
    rows = tile.shape[0]
    shift = shift % rows
    if rows % 8 == 0:
        return pltpu.roll(tile, shift, 0)
    return jnp.concatenate([tile[rows - shift :], tile[: rows - shift]], axis=0)


def lane_index(rows):
    return lax.broadcasted_iota(jnp.int32, (rows, LANES), 1)


def pack_kernel(
    plan, state_hbm, mean_hbm, *refs
):
    lookups_hbm, (message, table), rest = refs[:5], refs[5:7], refs[7:]
    lookups, rest = rest[:5], rest[5:]
    state, mean, filled, les_inv, ac_inv, pair_inv, small_sem, state_sem, mean_sem = rest
    les_owner, ac_owner, les_nbr, ac_nbr, coupling = lookups
    small = [
        pltpu.make_async_copy(source, target, small_sem.at[i])
        for i, (source, target) in enumerate(zip(lookups_hbm, lookups))
    ]
    for copy in small:
        copy.start()
    large = []
    for v in range(plan.vars):
        large.append(pltpu.make_async_copy(state_hbm.at[v], state.at[v], state_sem.at[v]))
        large.append(pltpu.make_async_copy(mean_hbm.at[v], mean.at[v], mean_sem.at[v]))
    for copy in large:
        copy.start()
    section = lax.axis_index("section")
    px, py = plan.own_piece(section, lax.axis_index("block"))
    for copy in small:
        copy.wait()
    look_up(plan, px, py, table, lookups, les_inv, ac_inv, pair_inv)
    for copy in large:
        copy.wait()

    xs, side, half = plan.xs, plan.side, plan.half
    width = side * side
    offsets = [jnp.where(section == 0, OFFSETS[0][v], OFFSETS[1][v]) for v in range(plan.vars)]
    for v in range(plan.vars):
        state[v] = (state[v] - offsets[v]) * SCALE_IN
    lane = lane_index(xs)
    for device in range(plan.devices):
        tx, ty = plan.piece(device)
        x0, l0 = tx * xs, ty * LANES
        here = slice(l0, l0 + LANES)
        before = (l0 - LANES) % width
        after = (l0 + LANES) % width
        for v in range(plan.vars):
            filled[device, v * xs : (v + 1) * xs, :] = state[v, x0 : x0 + xs, here]
            filled[device, plan.x_base + v, :] = state[v, (x0 - 1) % side, here]
            filled[device, plan.x_base + plan.vars + v, :] = state[v, (x0 + xs) % side, here]
            first, second = mean[v, x0 : x0 + half, here], mean[v, x0 + half : x0 + xs, here]
            piece = jnp.where(section == 0, first, second)
            base = plan.mean_base + v * half
            filled[device, base : base + half, :] = (piece - MEAN_OFFSETS[v]) * SCALE_IN
        for i, (a, b) in enumerate(PAIRS):
            edge = [
                jnp.where(
                    lane >= LANES - side,
                    state[v, x0 : x0 + xs, before : before + LANES],
                    state[v, x0 : x0 + xs, after : after + LANES],
                )
                for v in ((a, b) if a != b else (a,))
            ]
            tile = edge[0]
            if a != b:
                outer = (lane < side) | (lane >= LANES - side)
                tile = jnp.where(outer, edge[0], roll_lanes(edge[1], LANES // 2))
            base = plan.y_base + i * xs
            filled[device, base : base + xs, :] = tile
        used = plan.x_base + 2 * plan.vars
        if used < plan.rows:
            filled[device, used:, :] = jnp.zeros((plan.rows - used, LANES), jnp.float32)
        message[device] = to_wire(filled[device])


def look_up(plan, px, py, table, lookups, les_inv, ac_inv, pair_inv):
    les_owner, ac_owner, les_nbr, ac_nbr, coupling = lookups
    for i in range(plan.blocks):
        les_inv[les_owner[i]] = i
        ac_inv[ac_owner[i]] = i
        pair_inv[coupling[i]] = i
    at_edge = (px == 0, px == plan.nx - 1, py == 0, py == plan.ny - 1, True, True)
    faces = FACES if plan.layers_z > 1 else 4
    for slot in range(plan.blocks):
        les_block = les_inv[slot]
        ac_block = ac_inv[slot]
        for kind, (block, nbr, owner) in enumerate(
            ((les_block, les_nbr, les_owner), (ac_block, ac_nbr, ac_owner))
        ):
            for face in range(FACES):
                if face < faces:
                    other = nbr[face, block]
                    source = jnp.where(other < 0, -1, owner[jnp.maximum(other, 0)])
                    if face < 4:
                        source = jnp.where(at_edge[face], source, slot)
                else:
                    source = -1
                table[(kind * COLUMNS + face) * plan.blocks + slot] = source
        table[FACES * plan.blocks + slot] = ac_owner[pair_inv[les_block]]
        table[(COLUMNS + FACES) * plan.blocks + slot] = les_owner[coupling[ac_block]]


def sides(plan, table, kind, slot, core, x_halo, y_halo):
    xs, side = plan.xs, plan.side
    lane = lane_index(xs)
    row = lax.broadcasted_iota(jnp.int32, (xs, LANES), 0)
    depth = lane % side
    faces = FACES if plan.layers_z > 1 else 4
    found = [table[(kind * COLUMNS + face) * plan.blocks + slot] for face in range(faces)]
    inside = [f >= 0 for f in found]
    found = [jnp.maximum(f, 0) for f in found]
    own = [core(kind, slot, v) for v in range(plan.vars)]
    shifted = [[] for _ in range(FACES)]
    for v, tile in enumerate(own):
        low = jnp.where(inside[0], x_halo(kind, found[0], v, 0), tile)
        high = jnp.where(inside[1], x_halo(kind, found[1], v, 1), tile)
        shifted[0].append(jnp.where(row == 0, low, roll_rows(tile, 1)))
        shifted[1].append(jnp.where(row == xs - 1, high, roll_rows(tile, -1)))
        low = roll_lanes(jnp.where(lane >= LANES - side, y_halo(kind, found[2], v, 0), tile), side)
        high = roll_lanes(jnp.where(lane < side, y_halo(kind, found[3], v, 1), tile), -side)
        shifted[2].append(jnp.where((lane < side) & ~inside[2], tile, low))
        shifted[3].append(jnp.where((lane >= LANES - side) & ~inside[3], tile, high))
        low, high = tile, tile
        if plan.layers_z > 1:
            low = jnp.where(inside[4], roll_lanes(core(kind, found[4], v), 1 - side), tile)
            high = jnp.where(inside[5], roll_lanes(core(kind, found[5], v), side - 1), tile)
        shifted[4].append(jnp.where(depth == 0, low, roll_lanes(tile, 1)))
        shifted[5].append(jnp.where(depth == side - 1, high, roll_lanes(tile, -1)))
    return own, shifted


def primitives(conserved):
    density, energy = conserved[0], conserved[4]
    momentum = conserved[1:4]
    inverse = 1.0 / density
    velocity = [m * inverse for m in momentum]
    kinetic = momentum[0] * velocity[0] + momentum[1] * velocity[1] + momentum[2] * velocity[2]
    return momentum, energy, velocity, GAMMA_LESS * (energy - 0.5 * kinetic)


def flux_along(conserved, axis):
    momentum, energy, velocity, pressure = primitives(conserved)
    normal = velocity[axis]
    flux = [momentum[axis]]
    for component in range(3):
        entry = momentum[component] * normal
        flux.append(entry + pressure if component == axis else entry)
    flux.append((energy + pressure) * normal)
    return flux, velocity


def cross(a, b):
    return [
        a[1] * b[2] - a[2] * b[1],
        a[2] * b[0] - a[0] * b[2],
        a[0] * b[1] - a[1] * b[0],
    ]


def as_bf16(tile):
    return tile.astype(jnp.bfloat16).astype(jnp.float32)


def les_slot(plan, own, shifted):
    count = plan.vars
    total = [(1.0 - 6.0 * DT_LES * VISCOSITY) * own[v] for v in range(count)]
    gradient = []
    for axis in range(3):
        low, high = shifted[2 * axis], shifted[2 * axis + 1]
        flux_low, speed_low = flux_along(low, axis)
        flux_high, speed_high = flux_along(high, axis)
        for v in range(count):
            total[v] = total[v] + (
                DT_LES * VISCOSITY * (low[v] + high[v]) - 0.5 * DT_LES * (flux_high[v] - flux_low[v])
            )
        gradient.append([0.5 * (h - w) for h, w in zip(speed_high, speed_low)])
    velocity = [m * (1.0 / own[0]) for m in own[1:4]]
    vorticity = [
        gradient[1][2] - gradient[2][1],
        gradient[2][0] - gradient[0][2],
        gradient[0][1] - gradient[1][0],
    ]
    return total, [as_bf16(t) for t in cross(vorticity, velocity)]


def ac_slot(plan, own, shifted, mean, source):
    slope = [
        [0.5 * (h - w) for h, w in zip(shifted[2 * axis + 1], shifted[2 * axis])] for axis in range(3)
    ]
    carried = [
        mean[1] * slope[0][v] + mean[2] * slope[1][v] + mean[3] * slope[2][v]
        for v in range(plan.vars)
    ]
    divergence = slope[0][1] + slope[1][2] + slope[2][3]
    inverse = 1.0 / mean[0]
    change = [carried[0] + mean[0] * divergence]
    for axis in range(3):
        change.append(carried[1 + axis] + slope[axis][4] * inverse + source[axis])
    change.append(carried[4] + 1.4 * mean[4] * divergence)
    return [g - DT_AC * c for g, c in zip(own, change)]


def advance(plan, table, core, x_halo, y_halo, mean, lamb, store):
    xs = plan.xs

    def les_body(slot, carry):
        own, shifted = sides(plan, table, 0, slot, core, x_halo, y_halo)
        total, vector = les_slot(plan, own, shifted)
        partner = table[FACES * plan.blocks + slot]
        for j in range(3):
            back = as_bf16(core(1, partner, 1 + j))
            total[1 + j] = total[1 + j] + DT_LES * FEEDBACK_GAIN * back
            lamb[slot, j * xs : (j + 1) * xs, :] = vector[j]
        store(0, slot, total)
        return carry

    def ac_body(slot, carry):
        own, shifted = sides(plan, table, 1, slot, core, x_halo, y_halo)
        partner = table[(COLUMNS + FACES) * plan.blocks + slot]
        source = [lamb[partner, j * xs : (j + 1) * xs, :] for j in range(3)]
        store(1, slot, ac_slot(plan, own, shifted, mean(slot), source))
        return carry

    lax.fori_loop(0, plan.blocks, les_body, 0, unroll=4)
    lax.fori_loop(0, plan.blocks, ac_body, 0, unroll=4)


def tile_rows(plan, v):
    return slice(v * plan.xs, (v + 1) * plan.xs)


def first_kernel(
    plan, table, message,
    after, mean_out, x_up, x_down, y_up, y_down,
    arrived, lamb, x_up_raw, x_down_raw, y_up_raw, y_down_raw,
):
    xs, side, count, blocks, half = plan.xs, plan.side, plan.vars, plan.blocks, plan.half
    lane = lane_index(xs)

    def read(m, carry):
        arrived[m] = from_wire(message[m]) * (1.0 / SCALE_IN)
        return carry

    lax.fori_loop(0, plan.devices, read, 0, unroll=2)

    def read_mean(slot, carry):
        for v in range(count):
            base = plan.mean_base + v * half
            for part in range(plan.devices // blocks):
                rows = arrived[part * blocks + slot, base : base + half, :]
                start = v * xs + part * half
                mean_out[slot, start : start + half, :] = rows + MEAN_OFFSETS[v]
        return carry

    lax.fori_loop(0, blocks, read_mean, 0)

    def shift_back(tile, kind, v):
        return tile if OFFSETS[kind][v] == 0.0 else tile + OFFSETS[kind][v]

    def core(kind, slot, v):
        return shift_back(arrived[kind * blocks + slot, tile_rows(plan, v), :], kind, v)

    def x_halo(kind, slot, v, end):
        at = plan.x_base + end * count + v
        return shift_back(arrived[kind * blocks + slot, at : at + 1, :], kind, v)

    def y_halo(kind, slot, v, end):
        base = plan.y_base + (v // 2) * xs
        tile = arrived[kind * blocks + slot, base : base + xs, :]
        if v % 2 == 1:
            tile = roll_lanes(tile, LANES // 2)
        return shift_back(tile, kind, v)

    def mean(slot):
        return [mean_out[slot, tile_rows(plan, v), :] for v in range(count)]

    def store(kind, slot, tiles):
        m = kind * blocks + slot
        quarter = m % 4
        rest = plan.devices * xs + (m // 4) * xs
        up = down = None
        for v, tile in enumerate(tiles):
            after[m, tile_rows(plan, v), :] = tile
            coded = (tile - OFFSETS[kind][v]) * SCALE_MID
            x_up_raw[pl.ds(m * count + v, 1), :] = coded[xs - 1 : xs]
            x_down_raw[pl.ds(m * count + v, 1), :] = coded[0:1]
            if v < 4:
                high = roll_lanes(coded, side * (v + 1))
                low = roll_lanes(coded, side * v)
                mine = lane >= side * v
                up = high if v == 0 else jnp.where(mine, high, up)
                down = low if v == 0 else jnp.where(mine, low, down)
            else:
                high = pltpu.roll(coded, (side * (quarter + 1)) % LANES, 1)
                low = pltpu.roll(coded, side * quarter, 1)
                mine = lane >= side * quarter
                where = pl.ds(pl.multiple_of(rest, xs), xs)
                y_up_raw[where, :] = jnp.where(mine, high, y_up_raw[where, :])
                y_down_raw[where, :] = jnp.where(mine, low, y_down_raw[where, :])
        where = pl.ds(pl.multiple_of(m * xs, xs), xs)
        y_up_raw[where, :] = up
        y_down_raw[where, :] = down

    advance(plan, table, core, x_halo, y_halo, mean, lamb, store)
    for raw, out in (
        (x_up_raw, x_up), (x_down_raw, x_down), (y_up_raw, y_up), (y_down_raw, y_down),
    ):
        out[...] = to_wire(raw[...])


def last_kernel(
    plan, table, before, mean_in, x_low, x_high, y_low, y_high,
    message, lamb, x_low_raw, x_high_raw, y_low_raw, y_high_raw, coded,
):
    xs, side, count, blocks = plan.xs, plan.side, plan.vars, plan.blocks
    for raw, sent in (
        (x_low_raw, x_low), (x_high_raw, x_high), (y_low_raw, y_low), (y_high_raw, y_high),
    ):
        raw[...] = from_wire(sent[...]) * (1.0 / SCALE_MID)

    def shift_back(tile, kind, v):
        return tile if OFFSETS[kind][v] == 0.0 else tile + OFFSETS[kind][v]

    def core(kind, slot, v):
        return before[kind * blocks + slot, tile_rows(plan, v), :]

    def x_halo(kind, slot, v, end):
        raw = x_high_raw if end else x_low_raw
        at = (kind * blocks + slot) * count + v
        return shift_back(raw[pl.ds(at, 1), :], kind, v)

    def y_halo(kind, slot, v, end):
        raw = y_high_raw if end else y_low_raw
        m = kind * blocks + slot
        target = 0 if end else 3 * side
        if v < 4:
            tile = raw[pl.ds(pl.multiple_of(m * xs, xs), xs), :]
            tile = roll_lanes(tile, target - side * v)
        else:
            rest = plan.devices * xs + (m // 4) * xs
            tile = raw[pl.ds(pl.multiple_of(rest, xs), xs), :]
            tile = pltpu.roll(tile, (target + LANES - side * (m % 4)) % LANES, 1)
        return shift_back(tile, kind, v)

    def mean(slot):
        return [mean_in[slot, tile_rows(plan, v), :] for v in range(count)]

    def store(kind, slot, tiles):
        for v, tile in enumerate(tiles):
            coded[kind * blocks + slot, tile_rows(plan, v), :] = (tile - OFFSETS[kind][v]) * SCALE_OUT

    advance(plan, table, core, x_halo, y_halo, mean, lamb, store)

    def write(m, carry):
        message[m] = to_wire(coded[m])
        return carry

    lax.fori_loop(0, plan.devices, write, 0, unroll=2)


def unpack_kernel(plan, message, out):
    section = lax.axis_index("section")
    xs = plan.xs
    for device in range(plan.devices):
        tx, ty = plan.piece(device)
        values = from_wire(message[device]) * (1.0 / SCALE_OUT)
        for v in range(plan.vars):
            offset = jnp.where(section == 0, OFFSETS[0][v], OFFSETS[1][v])
            out[v, tx * xs : (tx + 1) * xs, ty * LANES : (ty + 1) * LANES] = (
                values[v * xs : (v + 1) * xs] + offset
            )


def vmem(count):
    return [pl.BlockSpec(memory_space=pltpu.VMEM)] * count


def smem(count):
    return [pl.BlockSpec(memory_space=pltpu.SMEM)] * count


def on_device(plan, state, mean_flow, les_owner, ac_owner, les_nbr, ac_nbr, coupling):
    axes = ("section", "block")
    devices, blocks, count, xs = plan.devices, plan.blocks, plan.vars, plan.xs
    f32 = jnp.float32

    def array(dtype, *shape):
        return jax.ShapeDtypeStruct(shape, dtype)

    far = [
        pltpu.with_memory_space_constraint(a, pltpu.HBM)
        for a in (state[0, 0], mean_flow[0], les_owner, ac_owner, les_nbr.T, ac_nbr.T, coupling)
    ]
    volume = pltpu.VMEM((count, plan.side, plan.side * plan.side), f32)
    lookups = [pltpu.SMEM(a.shape, jnp.int32) for a in far[2:]]
    message, table = pl.pallas_call(
        functools.partial(pack_kernel, plan),
        out_shape=(
            array(WIRE, devices, plan.rows, LANES),
            array(jnp.int32, 2 * COLUMNS * blocks),
        ),
        in_specs=[pl.BlockSpec(memory_space=pltpu.HBM)] * len(far),
        out_specs=tuple(vmem(1) + smem(1)),
        scratch_shapes=lookups
        + [volume, volume, pltpu.VMEM((devices, plan.rows, LANES), f32)]
        + [pltpu.SMEM((blocks,), jnp.int32)] * 3
        + [pltpu.SemaphoreType.DMA((n,)) for n in (len(lookups), count, count)],
        name="pack",
        compiler_params=pltpu.CompilerParams(vmem_limit_bytes=16 * 1024 * 1024),
    )(*far)
    message = lax.all_to_all(message, axes, split_axis=0, concat_axis=0, tiled=True)

    x_rows = devices * count
    y_rows = devices * xs + devices // 4 * xs
    halo_shapes = [(x_rows, LANES)] * 2 + [(y_rows, LANES)] * 2
    halo_scratch = [pltpu.VMEM(shape, f32) for shape in halo_shapes]
    lamb_scratch = pltpu.VMEM((blocks, 3 * xs, LANES), f32)
    after, mean, *halos = pl.pallas_call(
        functools.partial(first_kernel, plan),
        out_shape=(
            array(f32, devices, plan.core_rows, LANES),
            array(f32, blocks, plan.core_rows, LANES),
            *(array(WIRE, *shape) for shape in halo_shapes),
        ),
        in_specs=smem(1) + vmem(1),
        out_specs=tuple(vmem(6)),
        scratch_shapes=[pltpu.VMEM((devices, plan.rows, LANES), f32), lamb_scratch] + halo_scratch,
        name="first_step",
        compiler_params=pltpu.CompilerParams(vmem_limit_bytes=16 * 1024 * 1024),
    )(table, message)
    moves = [plan.permutation(*step) for step in ((1, 0), (-1, 0), (0, 1), (0, -1))]
    halos = [lax.ppermute(halo, axes, move) for halo, move in zip(halos, moves)]

    message = pl.pallas_call(
        functools.partial(last_kernel, plan),
        out_shape=array(WIRE, devices, plan.core_rows, LANES),
        in_specs=smem(1) + vmem(6),
        out_specs=vmem(1)[0],
        scratch_shapes=[lamb_scratch]
        + halo_scratch
        + [pltpu.VMEM((devices, plan.core_rows, LANES), f32)],
        name="last_step",
        compiler_params=pltpu.CompilerParams(vmem_limit_bytes=16 * 1024 * 1024),
    )(table, after, mean, *halos)
    message = lax.all_to_all(message, axes, split_axis=0, concat_axis=0, tiled=True)

    result = pl.pallas_call(
        functools.partial(unpack_kernel, plan),
        out_shape=array(f32, *state.shape[2:]),
        in_specs=vmem(1),
        out_specs=vmem(1)[0],
        name="unpack",
        compiler_params=pltpu.CompilerParams(vmem_limit_bytes=16 * 1024 * 1024),
    )(message)
    return result[None, None]


def solution(mesh):
    def program(state, mean_flow, les_owner, ac_owner, les_nbr, ac_nbr, coupling):
        plan = Plan(mesh.shape["block"], mesh.shape["section"], state.shape[2], state.shape[3])
        return jax.shard_map(
            functools.partial(on_device, plan),
            mesh=mesh,
            in_specs=(
                P("section", "block", None, None, None),
                P("block", None, None, None),
                P(),
                P(),
                P(),
                P(),
                P(),
            ),
            out_specs=P("section", "block", None, None, None),
            check_vma=False,
        )(state, mean_flow, les_owner, ac_owner, les_nbr, ac_nbr, coupling)

    return program
```

```python
import functools

import jax
import jax.numpy as jnp
from jax import lax
from jax.experimental import pallas as pl
from jax.experimental.pallas import tpu as pltpu
from jax.sharding import PartitionSpec as P


STEPS = 2

GAMMA_LESS = 0.4
DT_LES = 0.2
DT_AC = 0.3
VISCOSITY = 0.05
FEEDBACK_GAIN = 0.5

WIRE = jnp.int16
SCALE_IN = 16384.0
SCALE_MID = 8192.0
SCALE_OUT = 4096.0
OFFSETS = ((1.25, 0.0, 0.0, 0.0, 2.6), (0.0, 0.0, 0.0, 0.0, 0.0))
MEAN_OFFSETS = (1.0, 0.0, 0.0, 0.0, 1.0)
PAIRS = ((0, 1), (2, 3), (4, 4))

LANES = 128
FACES = 6
COLUMNS = FACES + 1


class Plan:
    def __init__(self, blocks, sections, num_vars, side):
        self.blocks = blocks
        self.devices = blocks * sections
        self.vars = num_vars
        self.side = side
        self.layers_z = blocks // 16
        self.ny = side * side // LANES
        self.nx = self.devices // self.ny
        self.xs = side // self.nx
        self.half = self.xs // sections
        self.core_rows = num_vars * self.xs
        self.y_base = self.core_rows
        self.mean_base = self.y_base + len(PAIRS) * self.xs
        self.x_base = self.mean_base + num_vars * self.half
        self.rows = -(-(self.x_base + 2 * num_vars) // 16) * 16
        assert sections == 2 and LANES == 4 * side and 2 * self.half * self.nx == side

    def piece(self, device):
        section, block = device // self.blocks, device % self.blocks
        low, mid, high = block % 2, block // 2 % 2, block // 4
        ring = section if low == 0 else 3 - section
        depth = high % 4
        return ring + 4 * (high // 4), depth if mid == 0 else 7 - depth

    def own_piece(self, section, block):
        low, mid, high = block % 2, block // 2 % 2, block // 4
        ring = jnp.where(low == 0, section, 3 - section)
        depth = high % 4
        return ring + 4 * (high // 4), jnp.where(mid == 0, depth, 7 - depth)

    def permutation(self, step_x, step_y):
        at = {self.piece(d): d for d in range(self.devices)}
        assert len(at) == self.devices
        pairs = []
        for device in range(self.devices):
            px, py = self.piece(device)
            pairs.append((device, at[((px + step_x) % self.nx, (py + step_y) % self.ny)]))
        return pairs


def to_wire(scaled):
    return lax.round(scaled, lax.RoundingMethod.TO_NEAREST_EVEN).astype(jnp.int32).astype(WIRE)


def from_wire(sent):
    return sent.astype(jnp.int32).astype(jnp.float32)


def roll_lanes(tile, shift):
    shift = shift % LANES
    return pltpu.roll(tile, shift, 1) if shift else tile


def roll_rows(tile, shift):
    rows = tile.shape[0]
    shift = shift % rows
    if rows % 8 == 0:
        return pltpu.roll(tile, shift, 0)
    return jnp.concatenate([tile[rows - shift :], tile[: rows - shift]], axis=0)


def lane_index(rows):
    return lax.broadcasted_iota(jnp.int32, (rows, LANES), 1)


def pack_kernel(
    plan, state_hbm, mean_hbm, *refs
):
    lookups_hbm, (message, table), rest = refs[:5], refs[5:7], refs[7:]
    lookups, rest = rest[:5], rest[5:]
    state, mean, filled, les_inv, ac_inv, pair_inv, small_sem, state_sem, mean_sem = rest
    les_owner, ac_owner, les_nbr, ac_nbr, coupling = lookups
    small = [
        pltpu.make_async_copy(source, target, small_sem.at[i])
        for i, (source, target) in enumerate(zip(lookups_hbm, lookups))
    ]
    for copy in small:
        copy.start()
    large = []
    for v in range(plan.vars):
        large.append(pltpu.make_async_copy(state_hbm.at[v], state.at[v], state_sem.at[v]))
        large.append(pltpu.make_async_copy(mean_hbm.at[v], mean.at[v], mean_sem.at[v]))
    for copy in large:
        copy.start()
    section = lax.axis_index("section")
    px, py = plan.own_piece(section, lax.axis_index("block"))
    for copy in small:
        copy.wait()
    look_up(plan, px, py, table, lookups, les_inv, ac_inv, pair_inv)
    for copy in large:
        copy.wait()

    xs, side, half = plan.xs, plan.side, plan.half
    width = side * side
    offsets = [jnp.where(section == 0, OFFSETS[0][v], OFFSETS[1][v]) for v in range(plan.vars)]
    for v in range(plan.vars):
        state[v] = (state[v] - offsets[v]) * SCALE_IN
    lane = lane_index(xs)
    for device in range(plan.devices):
        tx, ty = plan.piece(device)
        x0, l0 = tx * xs, ty * LANES
        here = slice(l0, l0 + LANES)
        before = (l0 - LANES) % width
        after = (l0 + LANES) % width
        for v in range(plan.vars):
            filled[device, v * xs : (v + 1) * xs, :] = state[v, x0 : x0 + xs, here]
            filled[device, plan.x_base + v, :] = state[v, (x0 - 1) % side, here]
            filled[device, plan.x_base + plan.vars + v, :] = state[v, (x0 + xs) % side, here]
            first, second = mean[v, x0 : x0 + half, here], mean[v, x0 + half : x0 + xs, here]
            piece = jnp.where(section == 0, first, second)
            base = plan.mean_base + v * half
            filled[device, base : base + half, :] = (piece - MEAN_OFFSETS[v]) * SCALE_IN
        for i, (a, b) in enumerate(PAIRS):
            edge = [
                jnp.where(
                    lane >= LANES - side,
                    state[v, x0 : x0 + xs, before : before + LANES],
                    state[v, x0 : x0 + xs, after : after + LANES],
                )
                for v in ((a, b) if a != b else (a,))
            ]
            tile = edge[0]
            if a != b:
                outer = (lane < side) | (lane >= LANES - side)
                tile = jnp.where(outer, edge[0], roll_lanes(edge[1], LANES // 2))
            base = plan.y_base + i * xs
            filled[device, base : base + xs, :] = tile
        used = plan.x_base + 2 * plan.vars
        if used < plan.rows:
            filled[device, used:, :] = jnp.zeros((plan.rows - used, LANES), jnp.float32)
        message[device] = to_wire(filled[device])


def look_up(plan, px, py, table, lookups, les_inv, ac_inv, pair_inv):
    les_owner, ac_owner, les_nbr, ac_nbr, coupling = lookups
    for i in range(plan.blocks):
        les_inv[les_owner[i]] = i
        ac_inv[ac_owner[i]] = i
        pair_inv[coupling[i]] = i
    at_edge = (px == 0, px == plan.nx - 1, py == 0, py == plan.ny - 1, True, True)
    faces = FACES if plan.layers_z > 1 else 4
    for slot in range(plan.blocks):
        les_block = les_inv[slot]
        ac_block = ac_inv[slot]
        for kind, (block, nbr, owner) in enumerate(
            ((les_block, les_nbr, les_owner), (ac_block, ac_nbr, ac_owner))
        ):
            for face in range(FACES):
                if face < faces:
                    other = nbr[face, block]
                    source = jnp.where(other < 0, -1, owner[jnp.maximum(other, 0)])
                    if face < 4:
                        source = jnp.where(at_edge[face], source, slot)
                else:
                    source = -1
                table[(kind * COLUMNS + face) * plan.blocks + slot] = source
        table[FACES * plan.blocks + slot] = ac_owner[pair_inv[les_block]]
        table[(COLUMNS + FACES) * plan.blocks + slot] = les_owner[coupling[ac_block]]


def sides_xy(plan, table, kind, slot, own, x_halo, y_halo):
    xs, side = plan.xs, plan.side
    lane = lane_index(xs)
    row = lax.broadcasted_iota(jnp.int32, (xs, LANES), 0)
    found = [table[(kind * COLUMNS + face) * plan.blocks + slot] for face in range(4)]
    inside = [f >= 0 for f in found]
    found = [jnp.maximum(f, 0) for f in found]
    shifted = [[] for _ in range(4)]
    for v, tile in enumerate(own):
        low = jnp.where(inside[0], x_halo(kind, found[0], v, 0), tile)
        high = jnp.where(inside[1], x_halo(kind, found[1], v, 1), tile)
        shifted[0].append(jnp.where(row == 0, low, roll_rows(tile, 1)))
        shifted[1].append(jnp.where(row == xs - 1, high, roll_rows(tile, -1)))
        low = roll_lanes(jnp.where(lane >= LANES - side, y_halo(kind, found[2], v, 0), tile), side)
        high = roll_lanes(jnp.where(lane < side, y_halo(kind, found[3], v, 1), tile), -side)
        shifted[2].append(jnp.where((lane < side) & ~inside[2], tile, low))
        shifted[3].append(jnp.where((lane >= LANES - side) & ~inside[3], tile, high))
    return shifted


def sides_z(plan, table, kind, slot, own, core):
    side = plan.side
    depth = lane_index(plan.xs) % side
    shifted = [[], []]
    if plan.layers_z > 1:
        found = [table[(kind * COLUMNS + face) * plan.blocks + slot] for face in (4, 5)]
        inside = [f >= 0 for f in found]
        found = [jnp.maximum(f, 0) for f in found]
    for v, tile in enumerate(own):
        low, high = tile, tile
        if plan.layers_z > 1:
            low = jnp.where(inside[0], roll_lanes(core(kind, found[0], v), 1 - side), tile)
            high = jnp.where(inside[1], roll_lanes(core(kind, found[1], v), side - 1), tile)
        shifted[0].append(jnp.where(depth == 0, low, roll_lanes(tile, 1)))
        shifted[1].append(jnp.where(depth == side - 1, high, roll_lanes(tile, -1)))
    return shifted


def primitives(conserved):
    density, energy = conserved[0], conserved[4]
    momentum = conserved[1:4]
    inverse = 1.0 / density
    velocity = [m * inverse for m in momentum]
    kinetic = momentum[0] * velocity[0] + momentum[1] * velocity[1] + momentum[2] * velocity[2]
    return momentum, energy, velocity, GAMMA_LESS * (energy - 0.5 * kinetic)


def flux_along(conserved, axis):
    momentum, energy, velocity, pressure = primitives(conserved)
    normal = velocity[axis]
    flux = [momentum[axis]]
    for component in range(3):
        entry = momentum[component] * normal
        flux.append(entry + pressure if component == axis else entry)
    flux.append((energy + pressure) * normal)
    return flux, velocity


def cross(a, b):
    return [
        a[1] * b[2] - a[2] * b[1],
        a[2] * b[0] - a[0] * b[2],
        a[0] * b[1] - a[1] * b[0],
    ]


def as_bf16(tile):
    return tile.astype(jnp.bfloat16).astype(jnp.float32)


def plus(total, term):
    return term if total is None else total + term


def les_axes(plan, total, axes, pairs):
    nearby, outflow = [None] * plan.vars, [None] * plan.vars
    gradient = []
    for axis, (low, high) in zip(axes, pairs):
        flux_low, speed_low = flux_along(low, axis)
        flux_high, speed_high = flux_along(high, axis)
        for v in range(plan.vars):
            nearby[v] = plus(nearby[v], low[v] + high[v])
            outflow[v] = plus(outflow[v], flux_high[v] - flux_low[v])
        gradient.append([h - w for h, w in zip(speed_high, speed_low)])
    near, out = 0.5 * DT_LES * VISCOSITY, 0.25 * DT_LES
    return [t + (near * n - out * o) for t, n, o in zip(total, nearby, outflow)], gradient


def les_z(plan, table, slot, core, unit):
    own = [core(0, slot, v) for v in range(plan.vars)]
    total = [(0.5 - 3.0 * DT_LES * VISCOSITY) * g for g in own]
    total, gradient = les_axes(plan, total, (2,), [sides_z(plan, table, 0, slot, own, core)])
    partner = table[FACES * plan.blocks + slot]
    for j in range(3):
        back = as_bf16(core(1, partner, 1 + j))
        total[1 + j] = total[1 + j] + (0.5 * DT_LES * FEEDBACK_GAIN) * back
    inverse = unit / own[0]
    return total + gradient[0][:2] + [m * inverse for m in own[1:4]]


def les_xy(plan, part, shifted):
    count = plan.vars
    pairs = [shifted[0:2], shifted[2:4]]
    total, (along_x, along_y) = les_axes(plan, part[:count], (0, 1), pairs)
    along_z, velocity = part[count : count + 2], part[count + 2 :]
    vorticity = [along_y[2] - along_z[1], along_z[0] - along_x[2], along_x[1] - along_y[0]]
    return total, [as_bf16(t) for t in cross(vorticity, velocity)]


def ac_axes(plan, total, axes, pairs, mean, source):
    slope = [[h - w for h, w in zip(high, low)] for low, high in pairs]
    change = [None] * plan.vars
    divergence = None
    for axis, s in zip(axes, slope):
        change = [plus(c, mean[1 + axis] * t) for c, t in zip(change, s)]
        divergence = plus(divergence, s[1 + axis])
    inverse = 1.0 / mean[0]
    for axis, s in zip(axes, slope):
        change[1 + axis] = change[1 + axis] + s[4] * inverse
    if source is not None:
        change[1:4] = [c + t for c, t in zip(change[1:4], source)]
    change[0] = change[0] + mean[0] * divergence
    change[4] = change[4] + 1.4 * mean[4] * divergence
    return [t - (0.25 * DT_AC) * c for t, c in zip(total, change)]


def ac_z(plan, table, slot, core, mean):
    own = [core(1, slot, v) for v in range(plan.vars)]
    pair = sides_z(plan, table, 1, slot, own, core)
    return ac_axes(plan, [0.5 * g for g in own], (2,), [pair], mean(slot), None)


def advance(plan, table, core, x_halo, y_halo, mean, lamb, les_part, ac_part, store):
    xs = plan.xs

    def les_quad(quad, carry):
        results = []
        for r in range(4):
            slot = quad * 4 + r
            own = [core(0, slot, v) for v in range(plan.vars)]
            shifted = sides_xy(plan, table, 0, slot, own, x_halo, y_halo)
            total, vector = les_xy(plan, les_part(slot), shifted)
            for j in range(3):
                lamb[slot, j * xs : (j + 1) * xs, :] = vector[j]
            results.append(total)
        store(0, quad, results)
        return carry

    def ac_quad(quad, carry):
        results = []
        for r in range(4):
            slot = quad * 4 + r
            own = [core(1, slot, v) for v in range(plan.vars)]
            shifted = sides_xy(plan, table, 1, slot, own, x_halo, y_halo)
            partner = table[(COLUMNS + FACES) * plan.blocks + slot]
            source = [lamb[partner, j * xs : (j + 1) * xs, :] for j in range(3)]
            pairs = [shifted[0:2], shifted[2:4]]
            results.append(ac_axes(plan, ac_part(slot), (0, 1), pairs, mean(slot), source))
        store(1, quad, results)
        return carry

    lax.fori_loop(0, plan.blocks // 4, les_quad, 0)
    lax.fori_loop(0, plan.blocks // 4, ac_quad, 0)


def tile_rows(plan, v):
    return slice(v * plan.xs, (v + 1) * plan.xs)


def first_kernel(
    plan, table, message,
    after, mean_out, x_up, x_down, y_up, y_down,
    arrived, origin, lamb, x_up_raw, x_down_raw, y_up_raw, y_down_raw,
):
    xs, side, count, blocks, half = plan.xs, plan.side, plan.vars, plan.blocks, plan.half
    lane = lane_index(xs)
    outer = (lane < side) | (lane >= LANES - side)

    for kind in range(2):
        origin[kind] = jnp.zeros((plan.rows, LANES), jnp.float32)
        for v, offset in enumerate(MEAN_OFFSETS):
            base = plan.mean_base + v * half
            origin[kind, base : base + half, :] = jnp.full((half, LANES), offset * SCALE_IN, jnp.float32)
        for v, offset in enumerate(OFFSETS[kind]):
            if offset == 0.0:
                continue
            level = jnp.full((xs, LANES), offset * SCALE_IN, jnp.float32)
            origin[kind, tile_rows(plan, v), :] = level
            for end in range(2):
                origin[kind, plan.x_base + end * count + v, :] = level[0]
            base = plan.y_base + (v // 2) * xs
            origin[kind, base : base + xs, :] = jnp.where(outer, level, 0.0)

    def read(slot, carry):
        for kind in range(2):
            arrived[kind * blocks + slot] = from_wire(message[kind * blocks + slot]) + origin[kind]
        return carry

    lax.fori_loop(0, blocks, read, 0, unroll=2)

    def read_mean(slot, carry):
        for v in range(count):
            base = plan.mean_base + v * half
            for part in range(plan.devices // blocks):
                rows = arrived[part * blocks + slot, base : base + half, :]
                start = v * xs + part * half
                mean_out[slot, start : start + half, :] = rows * (1.0 / SCALE_IN)
        return carry

    lax.fori_loop(0, blocks, read_mean, 0, unroll=4)

    def core(kind, slot, v):
        return arrived[kind * blocks + slot, tile_rows(plan, v), :]

    def x_halo(kind, slot, v, end):
        at = plan.x_base + end * count + v
        return arrived[kind * blocks + slot, pl.ds(at, xs, stride=0), :]

    def y_halo(kind, slot, v, end):
        base = plan.y_base + (v // 2) * xs
        tile = arrived[kind * blocks + slot, base : base + xs, :]
        return roll_lanes(tile, LANES // 2) if v % 2 == 1 else tile

    def mean(slot):
        return [mean_out[slot, tile_rows(plan, v), :] for v in range(count)]

    def in_quarters(tiles, first):
        packed = None
        for quarter, tile in enumerate(tiles):
            moved = roll_lanes(tile, side * (quarter - first))
            packed = moved if packed is None else jnp.where(lane >= side * quarter, moved, packed)
        return packed

    def store(kind, quad, results):
        rest = []
        for r, tiles in enumerate(results):
            m = kind * blocks + quad * 4 + r
            coded = []
            for v, tile in enumerate(tiles):
                after[m, tile_rows(plan, v), :] = tile
                offset = OFFSETS[kind][v] * SCALE_MID
                coded.append(tile if offset == 0.0 else tile - offset)
                x_up_raw[pl.ds(m * count + v, 1), :] = coded[v][xs - 1 : xs]
                x_down_raw[pl.ds(m * count + v, 1), :] = coded[v][0:1]
            rest.append(coded[4])
            where = pl.ds(pl.multiple_of(m * xs, xs), xs)
            y_up_raw[where, :] = in_quarters(coded[:4], 3)
            y_down_raw[where, :] = in_quarters(coded[:4], 0)
        start = (plan.devices + kind * (blocks // 4) + quad) * xs
        where = pl.ds(pl.multiple_of(start, xs), xs)
        y_up_raw[where, :] = in_quarters(rest, 3)
        y_down_raw[where, :] = in_quarters(rest, 0)

    def les_part(slot):
        return les_z(plan, table, slot, core, SCALE_IN)

    def ac_part(slot):
        return ac_z(plan, table, slot, core, mean)

    advance(plan, table, core, x_halo, y_halo, mean, lamb, les_part, ac_part, store)
    for raw, out in (
        (x_up_raw, x_up), (x_down_raw, x_down), (y_up_raw, y_up), (y_down_raw, y_down),
    ):
        out[...] = to_wire(raw[...])


def middle_kernel(plan, table, before, mean_in, les_out, ac_out):
    def core(kind, slot, v):
        return before[kind * plan.blocks + slot, tile_rows(plan, v), :]

    def mean(slot):
        return [mean_in[slot, tile_rows(plan, v), :] for v in range(plan.vars)]

    def body(slot, carry):
        for i, tile in enumerate(les_z(plan, table, slot, core, SCALE_MID)):
            les_out[slot, tile_rows(plan, i), :] = tile
        for v, tile in enumerate(ac_z(plan, table, slot, core, mean)):
            ac_out[slot, tile_rows(plan, v), :] = tile
        return carry

    lax.fori_loop(0, plan.blocks, body, 0, unroll=2)


def last_kernel(
    plan, table, before, mean_in, les_in, ac_in, x_low, x_high, y_low, y_high,
    message, lamb, x_low_raw, x_high_raw, y_low_raw, y_high_raw, coded,
):
    xs, side, count, blocks = plan.xs, plan.side, plan.vars, plan.blocks
    for raw, sent in (
        (x_low_raw, x_low), (x_high_raw, x_high), (y_low_raw, y_low), (y_high_raw, y_high),
    ):
        raw[...] = from_wire(sent[...])

    def shift_back(tile, kind, v):
        offset = OFFSETS[kind][v] * SCALE_MID
        return tile if offset == 0.0 else tile + offset

    def core(kind, slot, v):
        return before[kind * blocks + slot, tile_rows(plan, v), :]

    def x_halo(kind, slot, v, end):
        raw = x_high_raw if end else x_low_raw
        at = (kind * blocks + slot) * count + v
        return shift_back(raw[pl.ds(at, xs, stride=0), :], kind, v)

    def y_halo(kind, slot, v, end):
        raw = y_high_raw if end else y_low_raw
        m = kind * blocks + slot
        target = 0 if end else 3 * side
        if v < 4:
            tile = raw[pl.ds(pl.multiple_of(m * xs, xs), xs), :]
            tile = roll_lanes(tile, target - side * v)
        else:
            rest = plan.devices * xs + (m >> 2) * xs
            tile = raw[pl.ds(pl.multiple_of(rest, xs), xs), :]
            tile = pltpu.roll(tile, (target + LANES - side * (m & 3)) & (LANES - 1), 1)
        return shift_back(tile, kind, v)

    def mean(slot):
        return [mean_in[slot, tile_rows(plan, v), :] for v in range(count)]

    def store(kind, quad, results):
        for r, tiles in enumerate(results):
            for v, tile in enumerate(tiles):
                offset = OFFSETS[kind][v] * SCALE_OUT
                tile = tile if offset == 0.0 else tile - offset
                coded[kind * blocks + quad * 4 + r, tile_rows(plan, v), :] = tile

    def les_part(slot):
        return [les_in[slot, tile_rows(plan, i), :] for i in range(count + 5)]

    def ac_part(slot):
        return [ac_in[slot, tile_rows(plan, v), :] for v in range(count)]

    advance(plan, table, core, x_halo, y_halo, mean, lamb, les_part, ac_part, store)

    def write(m, carry):
        message[m] = to_wire(coded[m])
        return carry

    lax.fori_loop(0, plan.devices, write, 0, unroll=4)


def unpack_kernel(plan, message, out):
    section = lax.axis_index("section")
    xs = plan.xs
    for device in range(plan.devices):
        tx, ty = plan.piece(device)
        values = from_wire(message[device]) * (1.0 / SCALE_OUT)
        for v in range(plan.vars):
            offset = jnp.where(section == 0, OFFSETS[0][v], OFFSETS[1][v])
            out[v, tx * xs : (tx + 1) * xs, ty * LANES : (ty + 1) * LANES] = (
                values[v * xs : (v + 1) * xs] + offset
            )


def vmem(count):
    return [pl.BlockSpec(memory_space=pltpu.VMEM)] * count


def smem(count):
    return [pl.BlockSpec(memory_space=pltpu.SMEM)] * count


def on_device(plan, state, mean_flow, les_owner, ac_owner, les_nbr, ac_nbr, coupling):
    axes = ("section", "block")
    devices, blocks, count, xs = plan.devices, plan.blocks, plan.vars, plan.xs
    f32 = jnp.float32

    def array(dtype, *shape):
        return jax.ShapeDtypeStruct(shape, dtype)

    far = [
        pltpu.with_memory_space_constraint(a, pltpu.HBM)
        for a in (state[0, 0], mean_flow[0], les_owner, ac_owner, les_nbr.T, ac_nbr.T, coupling)
    ]
    volume = pltpu.VMEM((count, plan.side, plan.side * plan.side), f32)
    lookups = [pltpu.SMEM(a.shape, jnp.int32) for a in far[2:]]
    message, table = pl.pallas_call(
        functools.partial(pack_kernel, plan),
        out_shape=(
            array(WIRE, devices, plan.rows, LANES),
            pltpu.SMEM((2 * COLUMNS * blocks,), jnp.int32),
        ),
        in_specs=[pl.BlockSpec(memory_space=pltpu.HBM)] * len(far),
        out_specs=tuple(vmem(1) + smem(1)),
        scratch_shapes=lookups
        + [volume, volume, pltpu.VMEM((devices, plan.rows, LANES), f32)]
        + [pltpu.SMEM((blocks,), jnp.int32)] * 3
        + [pltpu.SemaphoreType.DMA((n,)) for n in (len(lookups), count, count)],
        name="pack",
        compiler_params=pltpu.CompilerParams(vmem_limit_bytes=16 * 1024 * 1024),
    )(*far)
    message = lax.all_to_all(message, axes, split_axis=0, concat_axis=0, tiled=True)

    x_rows = devices * count
    y_rows = devices * xs + devices // 4 * xs
    halo_shapes = [(x_rows, LANES)] * 2 + [(y_rows, LANES)] * 2
    halo_scratch = [pltpu.VMEM(shape, f32) for shape in halo_shapes]
    lamb_scratch = pltpu.VMEM((blocks, 3 * xs, LANES), f32)
    after, mean, *halos = pl.pallas_call(
        functools.partial(first_kernel, plan),
        out_shape=(
            array(f32, devices, plan.core_rows, LANES),
            array(f32, blocks, plan.core_rows, LANES),
            *(array(WIRE, *shape) for shape in halo_shapes),
        ),
        in_specs=smem(1) + vmem(1),
        out_specs=tuple(vmem(6)),
        scratch_shapes=[
            pltpu.VMEM((devices, plan.rows, LANES), f32),
            pltpu.VMEM((2, plan.rows, LANES), f32),
            lamb_scratch,
        ]
        + halo_scratch,
        name="first_step",
        compiler_params=pltpu.CompilerParams(vmem_limit_bytes=16 * 1024 * 1024),
    )(table, message)
    moves = [plan.permutation(*step) for step in ((1, 0), (-1, 0), (0, 1), (0, -1))]
    halos = [lax.ppermute(halo, axes, move) for halo, move in zip(halos, moves)]

    parts = pl.pallas_call(
        functools.partial(middle_kernel, plan),
        out_shape=(
            array(f32, blocks, (count + 5) * xs, LANES),
            array(f32, blocks, plan.core_rows, LANES),
        ),
        in_specs=smem(1) + vmem(2),
        out_specs=tuple(vmem(2)),
        name="middle",
        compiler_params=pltpu.CompilerParams(vmem_limit_bytes=16 * 1024 * 1024),
    )(table, after, mean)
    message = pl.pallas_call(
        functools.partial(last_kernel, plan),
        out_shape=array(WIRE, devices, plan.core_rows, LANES),
        in_specs=smem(1) + vmem(8),
        out_specs=vmem(1)[0],
        scratch_shapes=[lamb_scratch]
        + halo_scratch
        + [pltpu.VMEM((devices, plan.core_rows, LANES), f32)],
        name="last_step",
        compiler_params=pltpu.CompilerParams(vmem_limit_bytes=16 * 1024 * 1024),
    )(table, after, mean, *parts, *halos)
    message = lax.all_to_all(message, axes, split_axis=0, concat_axis=0, tiled=True)

    result = pl.pallas_call(
        functools.partial(unpack_kernel, plan),
        out_shape=array(f32, *state.shape[2:]),
        in_specs=vmem(1),
        out_specs=vmem(1)[0],
        name="unpack",
        compiler_params=pltpu.CompilerParams(vmem_limit_bytes=16 * 1024 * 1024),
    )(message)
    return result[None, None]


def solution(mesh):
    def program(state, mean_flow, les_owner, ac_owner, les_nbr, ac_nbr, coupling):
        plan = Plan(mesh.shape["block"], mesh.shape["section"], state.shape[2], state.shape[3])
        return jax.shard_map(
            functools.partial(on_device, plan),
            mesh=mesh,
            in_specs=(
                P("section", "block", None, None, None),
                P("block", None, None, None),
                P(),
                P(),
                P(),
                P(),
                P(),
            ),
            out_specs=P("section", "block", None, None, None),
            check_vma=False,
        )(state, mean_flow, les_owner, ac_owner, les_nbr, ac_nbr, coupling)

    return program
```

```python
import functools

import jax
import jax.numpy as jnp
from jax import lax
from jax.experimental import pallas as pl
from jax.experimental.pallas import tpu as pltpu
from jax.sharding import PartitionSpec as P


STEPS = 2

GAMMA_LESS = 0.4
DT_LES = 0.2
DT_AC = 0.3
VISCOSITY = 0.05
FEEDBACK_GAIN = 0.5

WIRE = jnp.int16
SCALE_IN = 16384.0
SCALE_MID = 8192.0
SCALE_OUT = 4096.0
OFFSETS = ((1.25, 0.0, 0.0, 0.0, 2.6), (0.0, 0.0, 0.0, 0.0, 0.0))
MEAN_OFFSETS = (1.0, 0.0, 0.0, 0.0, 1.0)
PAIRS = ((0, 1), (2, 3), (4, 4))

LANES = 128
FACES = 6
COLUMNS = FACES + 1


class Plan:
    def __init__(self, blocks, sections, num_vars, side):
        self.blocks = blocks
        self.devices = blocks * sections
        self.vars = num_vars
        self.side = side
        self.layers_z = blocks // 16
        self.ny = side * side // LANES
        self.nx = self.devices // self.ny
        self.xs = side // self.nx
        self.half = self.xs // sections
        self.core_rows = num_vars * self.xs
        self.y_base = self.core_rows
        self.mean_base = self.y_base + len(PAIRS) * self.xs
        self.x_base = self.mean_base + num_vars * self.half
        self.rows = -(-(self.x_base + 2 * num_vars) // 16) * 16
        assert self.nx > 1 and sections == 2 and LANES == 4 * side and 2 * self.half * self.nx == side

    def piece(self, device):
        section, block = device // self.blocks, device % self.blocks
        low, mid, high = block % 2, block // 2 % 2, block // 4
        ring = section if low == 0 else 3 - section
        depth = high % 4
        return ring + 4 * (high // 4), depth if mid == 0 else 7 - depth

    def own_piece(self, section, block):
        low, mid, high = block % 2, block // 2 % 2, block // 4
        ring = jnp.where(low == 0, section, 3 - section)
        depth = high % 4
        return ring + 4 * (high // 4), jnp.where(mid == 0, depth, 7 - depth)

    def permutation(self, step_x, step_y):
        at = {self.piece(d): d for d in range(self.devices)}
        assert len(at) == self.devices
        pairs = []
        for device in range(self.devices):
            px, py = self.piece(device)
            pairs.append((device, at[((px + step_x) % self.nx, (py + step_y) % self.ny)]))
        return pairs


def to_wire(scaled):
    return lax.round(scaled, lax.RoundingMethod.TO_NEAREST_EVEN).astype(jnp.int32).astype(WIRE)


def from_wire(sent):
    return sent.astype(jnp.int32).astype(jnp.float32)


def roll_lanes(tile, shift):
    shift = shift % LANES
    return pltpu.roll(tile, shift, 1) if shift else tile


def roll_rows(tile, shift):
    rows = tile.shape[0]
    shift = shift % rows
    if rows % 8 == 0:
        return pltpu.roll(tile, shift, 0)
    return jnp.concatenate([tile[rows - shift :], tile[: rows - shift]], axis=0)


def lane_index(rows):
    return lax.broadcasted_iota(jnp.int32, (rows, LANES), 1)


def pack_kernel(
    plan, state_hbm, mean_hbm, *refs
):
    lookups_hbm, (message, table), rest = refs[:5], refs[5:7], refs[7:]
    lookups, rest = rest[:5], rest[5:]
    state, mean, filled, *found = rest[:-3]
    small_sem, state_sem, mean_sem = rest[-3:]
    small = [
        pltpu.make_async_copy(source, target, small_sem.at[i])
        for i, (source, target) in enumerate(zip(lookups_hbm, lookups))
    ]
    for copy in small:
        copy.start()
    large = []
    for v in range(plan.vars):
        large.append(pltpu.make_async_copy(state_hbm.at[v], state.at[v], state_sem.at[v]))
        large.append(pltpu.make_async_copy(mean_hbm.at[v], mean.at[v], mean_sem.at[v]))
    for copy in large:
        copy.start()
    section = lax.axis_index("section")
    px, py = plan.own_piece(section, lax.axis_index("block"))
    for copy in small:
        copy.wait()
    invert(plan, lookups, *found)

    xs, side, half = plan.xs, plan.side, plan.half
    width = side * side
    lane = lane_index(xs)
    outer = (lane < side) | (lane >= LANES - side)
    pieces = []
    for device in range(plan.devices):
        tx, ty = plan.piece(device)
        pieces.append((device, tx * xs, ty * LANES))
    whole = xs % 8 == 0
    gathered = plan.mean_base if whole else 0

    def put(device, start, tile):
        if whole:
            message[device, start : start + xs, :] = to_wire(tile)
        else:
            filled[device, start : start + xs, :] = tile

    used = plan.x_base + 2 * plan.vars
    for v in range(plan.vars):
        large[2 * v].wait()
        for slot in range(v * plan.blocks // plan.vars, (v + 1) * plan.blocks // plan.vars):
            look_up(plan, px, py, table, lookups, *found, slot)
        offset = jnp.where(section == 0, OFFSETS[0][v], OFFSETS[1][v])
        state[v] = (state[v] - offset) * SCALE_IN
        for device, x0, l0 in pieces:
            here = slice(l0, l0 + LANES)
            put(device, v * xs, state[v, x0 : x0 + xs, here])
            filled[device, plan.x_base + v, :] = state[v, (x0 - 1) % side, here]
            filled[device, plan.x_base + plan.vars + v, :] = state[v, (x0 + xs) % side, here]
        if v % 2 == 1 or v == plan.vars - 1:
            i, (a, b) = v // 2, PAIRS[v // 2]
            for device, x0, l0 in pieces:
                before = (l0 - LANES) % width
                after = (l0 + LANES) % width
                edge = [
                    jnp.where(
                        lane >= LANES - side,
                        state[u, x0 : x0 + xs, before : before + LANES],
                        state[u, x0 : x0 + xs, after : after + LANES],
                    )
                    for u in ((a, b) if a != b else (a,))
                ]
                tile = edge[0]
                if a != b:
                    tile = jnp.where(outer, edge[0], roll_lanes(edge[1], LANES // 2))
                put(device, plan.y_base + i * xs, tile)
        large[2 * v + 1].wait()
        for device, x0, l0 in pieces:
            here = slice(l0, l0 + LANES)
            first, second = mean[v, x0 : x0 + half, here], mean[v, x0 + half : x0 + xs, here]
            piece = jnp.where(section == 0, first, second)
            base = plan.mean_base + v * half
            filled[device, base : base + half, :] = (piece - MEAN_OFFSETS[v]) * SCALE_IN
    for device, _, _ in pieces:
        if used < plan.rows:
            filled[device, used:, :] = jnp.zeros((plan.rows - used, LANES), jnp.float32)
        message[device, gathered:, :] = to_wire(filled[device, gathered:, :])


def invert(plan, lookups, les_inv, ac_inv, pair_inv, les_slots, ac_slots):
    les_owner, ac_owner, _, _, coupling = lookups
    les_slots[0] = -1
    ac_slots[0] = -1
    for i in range(plan.blocks):
        les, ac = les_owner[i], ac_owner[i]
        les_inv[les] = i
        ac_inv[ac] = i
        les_slots[i + 1] = les
        ac_slots[i + 1] = ac
        pair_inv[coupling[i]] = i


def look_up(plan, px, py, table, lookups, les_inv, ac_inv, pair_inv, les_slots, ac_slots, slot):
    les_owner, ac_owner, les_nbr, ac_nbr, coupling = lookups
    les_block = les_inv[slot]
    ac_block = ac_inv[slot]
    for kind, (block, nbr, slots) in enumerate(
        ((les_block, les_nbr, les_slots), (ac_block, ac_nbr, ac_slots))
    ):

        def write(face, value):
            table[(kind * COLUMNS + face) * plan.blocks + slot] = value

        for axis, (at, count) in enumerate(((px, plan.nx), (py, plan.ny))):
            low, high = at == 0, at == count - 1
            source = slots[nbr[jnp.where(low, 2 * axis, 2 * axis + 1), block] + 1]
            write(2 * axis, jnp.where(low, source, slot))
            write(2 * axis + 1, jnp.where(high, source, slot))
        if plan.layers_z > 1:
            for face in (4, 5):
                write(face, slots[nbr[face, block] + 1])
    table[FACES * plan.blocks + slot] = ac_owner[pair_inv[les_block]]
    table[(COLUMNS + FACES) * plan.blocks + slot] = les_owner[coupling[ac_block]]


def sides_xy(plan, table, kind, slot, own, x_halo, y_halo):
    xs, side = plan.xs, plan.side
    lane = lane_index(xs)
    row = lax.broadcasted_iota(jnp.int32, (xs, LANES), 0)
    found = [table[(kind * COLUMNS + face) * plan.blocks + slot] for face in range(4)]
    inside = [f >= 0 for f in found]
    found = [jnp.maximum(f, 0) for f in found]
    shifted = [[] for _ in range(4)]
    for v, tile in enumerate(own):
        low = jnp.where(inside[0], x_halo(kind, found[0], v, 0), tile)
        high = jnp.where(inside[1], x_halo(kind, found[1], v, 1), tile)
        shifted[0].append(jnp.where(row == 0, low, roll_rows(tile, 1)))
        shifted[1].append(jnp.where(row == xs - 1, high, roll_rows(tile, -1)))
        low = roll_lanes(jnp.where(lane >= LANES - side, y_halo(kind, found[2], v, 0), tile), side)
        high = roll_lanes(jnp.where(lane < side, y_halo(kind, found[3], v, 1), tile), -side)
        shifted[2].append(jnp.where((lane < side) & ~inside[2], tile, low))
        shifted[3].append(jnp.where((lane >= LANES - side) & ~inside[3], tile, high))
    return shifted


def sides_z(plan, table, kind, slot, own, core):
    side = plan.side
    depth = lane_index(plan.xs) % side
    shifted = [[], []]
    if plan.layers_z > 1:
        found = [table[(kind * COLUMNS + face) * plan.blocks + slot] for face in (4, 5)]
        inside = [f >= 0 for f in found]
        found = [jnp.maximum(f, 0) for f in found]
    for v, tile in enumerate(own):
        low, high = tile, tile
        if plan.layers_z > 1:
            low = jnp.where(inside[0], roll_lanes(core(kind, found[0], v), 1 - side), tile)
            high = jnp.where(inside[1], roll_lanes(core(kind, found[1], v), side - 1), tile)
        shifted[0].append(jnp.where(depth == 0, low, roll_lanes(tile, 1)))
        shifted[1].append(jnp.where(depth == side - 1, high, roll_lanes(tile, -1)))
    return shifted


def primitives(conserved):
    density, energy = conserved[0], conserved[4]
    momentum = conserved[1:4]
    inverse = 1.0 / density
    velocity = [m * inverse for m in momentum]
    kinetic = momentum[0] * velocity[0] + momentum[1] * velocity[1] + momentum[2] * velocity[2]
    return momentum, energy, velocity, GAMMA_LESS * (energy - 0.5 * kinetic)


def flux_along(conserved, axis):
    momentum, energy, velocity, pressure = primitives(conserved)
    normal = velocity[axis]
    flux = [momentum[axis]]
    for component in range(3):
        entry = momentum[component] * normal
        flux.append(entry + pressure if component == axis else entry)
    flux.append((energy + pressure) * normal)
    return flux, velocity


def cross(a, b):
    return [
        a[1] * b[2] - a[2] * b[1],
        a[2] * b[0] - a[0] * b[2],
        a[0] * b[1] - a[1] * b[0],
    ]


def as_bf16(tile):
    return tile.astype(jnp.bfloat16).astype(jnp.float32)


def plus(total, term):
    return term if total is None else total + term


def les_axes(plan, total, axes, pairs):
    nearby, outflow = [None] * plan.vars, [None] * plan.vars
    gradient = []
    for axis, (low, high) in zip(axes, pairs):
        flux_low, speed_low = flux_along(low, axis)
        flux_high, speed_high = flux_along(high, axis)
        for v in range(plan.vars):
            nearby[v] = plus(nearby[v], low[v] + high[v])
            outflow[v] = plus(outflow[v], flux_high[v] - flux_low[v])
        gradient.append([h - w for h, w in zip(speed_high, speed_low)])
    near, out = 0.5 * DT_LES * VISCOSITY, 0.25 * DT_LES
    return [t + (near * n - out * o) for t, n, o in zip(total, nearby, outflow)], gradient


def les_z(plan, table, slot, core, unit):
    own = [core(0, slot, v) for v in range(plan.vars)]
    total = [(0.5 - 3.0 * DT_LES * VISCOSITY) * g for g in own]
    total, gradient = les_axes(plan, total, (2,), [sides_z(plan, table, 0, slot, own, core)])
    partner = table[FACES * plan.blocks + slot]
    for j in range(3):
        back = as_bf16(core(1, partner, 1 + j))
        total[1 + j] = total[1 + j] + (0.5 * DT_LES * FEEDBACK_GAIN) * back
    inverse = unit / own[0]
    return total + gradient[0][:2] + [m * inverse for m in own[1:4]]


def les_xy(plan, part, shifted):
    count = plan.vars
    pairs = [shifted[0:2], shifted[2:4]]
    total, (along_x, along_y) = les_axes(plan, part[:count], (0, 1), pairs)
    along_z, velocity = part[count : count + 2], part[count + 2 :]
    vorticity = [along_y[2] - along_z[1], along_z[0] - along_x[2], along_x[1] - along_y[0]]
    return total, [as_bf16(t) for t in cross(vorticity, velocity)]


def ac_axes(plan, total, axes, pairs, mean, source):
    slope = [[h - w for h, w in zip(high, low)] for low, high in pairs]
    change = [None] * plan.vars
    divergence = None
    for axis, s in zip(axes, slope):
        change = [plus(c, mean[1 + axis] * t) for c, t in zip(change, s)]
        divergence = plus(divergence, s[1 + axis])
    inverse = 1.0 / mean[0]
    for axis, s in zip(axes, slope):
        change[1 + axis] = change[1 + axis] + s[4] * inverse
    if source is not None:
        change[1:4] = [c + t for c, t in zip(change[1:4], source)]
    change[0] = change[0] + mean[0] * divergence
    change[4] = change[4] + 1.4 * mean[4] * divergence
    return [t - (0.25 * DT_AC) * c for t, c in zip(total, change)]


def ac_z(plan, table, slot, core, mean):
    own = [core(1, slot, v) for v in range(plan.vars)]
    pair = sides_z(plan, table, 1, slot, own, core)
    return ac_axes(plan, [0.5 * g for g in own], (2,), [pair], mean(slot), None)


def advance(plan, table, core, x_halo, y_halo, mean, lamb, les_part, ac_part, store):
    xs = plan.xs

    def les_quad(quad, carry):
        results = []
        for r in range(4):
            slot = quad * 4 + r
            own = [core(0, slot, v) for v in range(plan.vars)]
            shifted = sides_xy(plan, table, 0, slot, own, x_halo, y_halo)
            total, vector = les_xy(plan, les_part(slot), shifted)
            for j in range(3):
                lamb[slot, j * xs : (j + 1) * xs, :] = vector[j]
            results.append(total)
        store(0, quad, results)
        return carry

    def ac_quad(quad, carry):
        results = []
        for r in range(4):
            slot = quad * 4 + r
            own = [core(1, slot, v) for v in range(plan.vars)]
            shifted = sides_xy(plan, table, 1, slot, own, x_halo, y_halo)
            partner = table[(COLUMNS + FACES) * plan.blocks + slot]
            source = [lamb[partner, j * xs : (j + 1) * xs, :] for j in range(3)]
            pairs = [shifted[0:2], shifted[2:4]]
            results.append(ac_axes(plan, ac_part(slot), (0, 1), pairs, mean(slot), source))
        store(1, quad, results)
        return carry

    lax.fori_loop(0, plan.blocks // 4, les_quad, 0)
    lax.fori_loop(0, plan.blocks // 4, ac_quad, 0)


def tile_rows(plan, v):
    return slice(v * plan.xs, (v + 1) * plan.xs)


def first_kernel(
    plan, table, message,
    after, mean_out, x_up, x_down, y_up, y_down,
    arrived, origin, lamb, x_up_raw, x_down_raw, y_up_raw, y_down_raw,
):
    xs, side, count, blocks, half = plan.xs, plan.side, plan.vars, plan.blocks, plan.half
    lane = lane_index(xs)
    outer = (lane < side) | (lane >= LANES - side)

    for kind in range(2):
        origin[kind] = jnp.zeros((plan.rows, LANES), jnp.float32)
        for v, offset in enumerate(MEAN_OFFSETS):
            base = plan.mean_base + v * half
            origin[kind, base : base + half, :] = jnp.full((half, LANES), offset * SCALE_IN, jnp.float32)
        for v, offset in enumerate(OFFSETS[kind]):
            if offset == 0.0:
                continue
            level = jnp.full((xs, LANES), offset * SCALE_IN, jnp.float32)
            origin[kind, tile_rows(plan, v), :] = level
            for end in range(2):
                origin[kind, plan.x_base + end * count + v, :] = level[0]
            base = plan.y_base + (v // 2) * xs
            origin[kind, base : base + xs, :] = jnp.where(outer, level, 0.0)

    def read(slot, carry):
        for kind in range(2):
            arrived[kind * blocks + slot] = from_wire(message[kind * blocks + slot]) + origin[kind]
        return carry

    lax.fori_loop(0, blocks, read, 0, unroll=2)

    def read_mean(slot, carry):
        for v in range(count):
            base = plan.mean_base + v * half
            for part in range(plan.devices // blocks):
                rows = arrived[part * blocks + slot, base : base + half, :]
                start = v * xs + part * half
                mean_out[slot, start : start + half, :] = rows * (1.0 / SCALE_IN)
        return carry

    lax.fori_loop(0, blocks, read_mean, 0, unroll=4)

    def core(kind, slot, v):
        return arrived[kind * blocks + slot, tile_rows(plan, v), :]

    def x_halo(kind, slot, v, end):
        at = plan.x_base + end * count + v
        return arrived[kind * blocks + slot, pl.ds(at, xs, stride=0), :]

    def y_halo(kind, slot, v, end):
        base = plan.y_base + (v // 2) * xs
        tile = arrived[kind * blocks + slot, base : base + xs, :]
        return roll_lanes(tile, LANES // 2) if v % 2 == 1 else tile

    def mean(slot):
        return [mean_out[slot, tile_rows(plan, v), :] for v in range(count)]

    def in_quarters(tiles, first):
        packed = None
        for quarter, tile in enumerate(tiles):
            moved = roll_lanes(tile, side * (quarter - first))
            packed = moved if packed is None else jnp.where(lane >= side * quarter, moved, packed)
        return packed

    def store(kind, quad, results):
        rest = []
        for r, tiles in enumerate(results):
            m = kind * blocks + quad * 4 + r
            coded = []
            for v, tile in enumerate(tiles):
                after[m, tile_rows(plan, v), :] = tile
                offset = OFFSETS[kind][v] * SCALE_MID
                coded.append(tile if offset == 0.0 else tile - offset)
                x_up_raw[pl.ds(m * count + v, 1), :] = coded[v][xs - 1 : xs]
                x_down_raw[pl.ds(m * count + v, 1), :] = coded[v][0:1]
            rest.append(coded[4])
            where = pl.ds(pl.multiple_of(m * xs, xs), xs)
            y_up_raw[where, :] = in_quarters(coded[:4], 3)
            y_down_raw[where, :] = in_quarters(coded[:4], 0)
        start = (plan.devices + kind * (blocks // 4) + quad) * xs
        where = pl.ds(pl.multiple_of(start, xs), xs)
        y_up_raw[where, :] = in_quarters(rest, 3)
        y_down_raw[where, :] = in_quarters(rest, 0)

    def les_part(slot):
        return les_z(plan, table, slot, core, SCALE_IN)

    def ac_part(slot):
        return ac_z(plan, table, slot, core, mean)

    advance(plan, table, core, x_halo, y_halo, mean, lamb, les_part, ac_part, store)
    for raw, out in (
        (x_up_raw, x_up), (x_down_raw, x_down), (y_up_raw, y_up), (y_down_raw, y_down),
    ):
        out[...] = to_wire(raw[...])


def middle_kernel(plan, table, before, mean_in, les_out, ac_out):
    def core(kind, slot, v):
        return before[kind * plan.blocks + slot, tile_rows(plan, v), :]

    def mean(slot):
        return [mean_in[slot, tile_rows(plan, v), :] for v in range(plan.vars)]

    def body(slot, carry):
        for i, tile in enumerate(les_z(plan, table, slot, core, SCALE_MID)):
            les_out[slot, tile_rows(plan, i), :] = tile
        for v, tile in enumerate(ac_z(plan, table, slot, core, mean)):
            ac_out[slot, tile_rows(plan, v), :] = tile
        return carry

    lax.fori_loop(0, plan.blocks, body, 0, unroll=2)


def last_kernel(
    plan, table, before, mean_in, les_in, ac_in, x_low, x_high, y_low, y_high,
    message, lamb, x_low_raw, x_high_raw, y_low_raw, y_high_raw, coded,
):
    xs, side, count, blocks = plan.xs, plan.side, plan.vars, plan.blocks
    for raw, sent in (
        (x_low_raw, x_low), (x_high_raw, x_high), (y_low_raw, y_low), (y_high_raw, y_high),
    ):
        raw[...] = from_wire(sent[...])

    def shift_back(tile, kind, v):
        offset = OFFSETS[kind][v] * SCALE_MID
        return tile if offset == 0.0 else tile + offset

    def core(kind, slot, v):
        return before[kind * blocks + slot, tile_rows(plan, v), :]

    def x_halo(kind, slot, v, end):
        raw = x_high_raw if end else x_low_raw
        at = (kind * blocks + slot) * count + v
        return shift_back(raw[pl.ds(at, xs, stride=0), :], kind, v)

    def y_halo(kind, slot, v, end):
        raw = y_high_raw if end else y_low_raw
        m = kind * blocks + slot
        target = 0 if end else 3 * side
        if v < 4:
            tile = raw[pl.ds(pl.multiple_of(m * xs, xs), xs), :]
            tile = roll_lanes(tile, target - side * v)
        else:
            rest = plan.devices * xs + (m >> 2) * xs
            tile = raw[pl.ds(pl.multiple_of(rest, xs), xs), :]
            tile = pltpu.roll(tile, (target + LANES - side * (m & 3)) & (LANES - 1), 1)
        return shift_back(tile, kind, v)

    def mean(slot):
        return [mean_in[slot, tile_rows(plan, v), :] for v in range(count)]

    def store(kind, quad, results):
        for r, tiles in enumerate(results):
            for v, tile in enumerate(tiles):
                offset = OFFSETS[kind][v] * SCALE_OUT
                tile = tile if offset == 0.0 else tile - offset
                coded[kind * blocks + quad * 4 + r, tile_rows(plan, v), :] = tile

    def les_part(slot):
        return [les_in[slot, tile_rows(plan, i), :] for i in range(count + 5)]

    def ac_part(slot):
        return [ac_in[slot, tile_rows(plan, v), :] for v in range(count)]

    advance(plan, table, core, x_halo, y_halo, mean, lamb, les_part, ac_part, store)

    def write(m, carry):
        message[m] = to_wire(coded[m])
        return carry

    lax.fori_loop(0, plan.devices, write, 0, unroll=4)


def unpack_kernel(plan, message, out):
    section = lax.axis_index("section")
    xs = plan.xs
    for device in range(plan.devices):
        tx, ty = plan.piece(device)
        values = from_wire(message[device]) * (1.0 / SCALE_OUT)
        for v in range(plan.vars):
            offset = jnp.where(section == 0, OFFSETS[0][v], OFFSETS[1][v])
            out[v, tx * xs : (tx + 1) * xs, ty * LANES : (ty + 1) * LANES] = (
                values[v * xs : (v + 1) * xs] + offset
            )


def vmem(count):
    return [pl.BlockSpec(memory_space=pltpu.VMEM)] * count


def smem(count):
    return [pl.BlockSpec(memory_space=pltpu.SMEM)] * count


def on_device(plan, state, mean_flow, les_owner, ac_owner, les_nbr, ac_nbr, coupling):
    axes = ("section", "block")
    devices, blocks, count, xs = plan.devices, plan.blocks, plan.vars, plan.xs
    f32 = jnp.float32

    def array(dtype, *shape):
        return jax.ShapeDtypeStruct(shape, dtype)

    far = [
        pltpu.with_memory_space_constraint(a, pltpu.HBM)
        for a in (state[0, 0], mean_flow[0], les_owner, ac_owner, les_nbr.T, ac_nbr.T, coupling)
    ]
    volume = pltpu.VMEM((count, plan.side, plan.side * plan.side), f32)
    lookups = [pltpu.SMEM(a.shape, jnp.int32) for a in far[2:]]
    message, table = pl.pallas_call(
        functools.partial(pack_kernel, plan),
        out_shape=(
            array(WIRE, devices, plan.rows, LANES),
            pltpu.SMEM((2 * COLUMNS * blocks,), jnp.int32),
        ),
        in_specs=[pl.BlockSpec(memory_space=pltpu.HBM)] * len(far),
        out_specs=tuple(vmem(1) + smem(1)),
        scratch_shapes=lookups
        + [volume, volume, pltpu.VMEM((devices, plan.rows, LANES), f32)]
        + [pltpu.SMEM((blocks,), jnp.int32)] * 3
        + [pltpu.SMEM((blocks + 1,), jnp.int32)] * 2
        + [pltpu.SemaphoreType.DMA((n,)) for n in (len(lookups), count, count)],
        name="pack",
        compiler_params=pltpu.CompilerParams(vmem_limit_bytes=16 * 1024 * 1024),
    )(*far)
    message = lax.all_to_all(message, axes, split_axis=0, concat_axis=0, tiled=True)

    x_rows = devices * count
    y_rows = devices * xs + devices // 4 * xs
    halo_shapes = [(x_rows, LANES)] * 2 + [(y_rows, LANES)] * 2
    halo_scratch = [pltpu.VMEM(shape, f32) for shape in halo_shapes]
    lamb_scratch = pltpu.VMEM((blocks, 3 * xs, LANES), f32)
    after, mean, *halos = pl.pallas_call(
        functools.partial(first_kernel, plan),
        out_shape=(
            array(f32, devices, plan.core_rows, LANES),
            array(f32, blocks, plan.core_rows, LANES),
            *(array(WIRE, *shape) for shape in halo_shapes),
        ),
        in_specs=smem(1) + vmem(1),
        out_specs=tuple(vmem(6)),
        scratch_shapes=[
            pltpu.VMEM((devices, plan.rows, LANES), f32),
            pltpu.VMEM((2, plan.rows, LANES), f32),
            lamb_scratch,
        ]
        + halo_scratch,
        name="first_step",
        compiler_params=pltpu.CompilerParams(vmem_limit_bytes=16 * 1024 * 1024),
    )(table, message)
    moves = [plan.permutation(*step) for step in ((1, 0), (-1, 0), (0, 1), (0, -1))]
    halos = [lax.ppermute(halo, axes, move) for halo, move in zip(halos, moves)]

    parts = pl.pallas_call(
        functools.partial(middle_kernel, plan),
        out_shape=(
            array(f32, blocks, (count + 5) * xs, LANES),
            array(f32, blocks, plan.core_rows, LANES),
        ),
        in_specs=smem(1) + vmem(2),
        out_specs=tuple(vmem(2)),
        name="middle",
        compiler_params=pltpu.CompilerParams(vmem_limit_bytes=16 * 1024 * 1024),
    )(table, after, mean)
    message = pl.pallas_call(
        functools.partial(last_kernel, plan),
        out_shape=array(WIRE, devices, plan.core_rows, LANES),
        in_specs=smem(1) + vmem(8),
        out_specs=vmem(1)[0],
        scratch_shapes=[lamb_scratch]
        + halo_scratch
        + [pltpu.VMEM((devices, plan.core_rows, LANES), f32)],
        name="last_step",
        compiler_params=pltpu.CompilerParams(vmem_limit_bytes=16 * 1024 * 1024),
    )(table, after, mean, *parts, *halos)
    message = lax.all_to_all(message, axes, split_axis=0, concat_axis=0, tiled=True)

    result = pl.pallas_call(
        functools.partial(unpack_kernel, plan),
        out_shape=array(f32, *state.shape[2:]),
        in_specs=vmem(1),
        out_specs=vmem(1)[0],
        name="unpack",
        compiler_params=pltpu.CompilerParams(vmem_limit_bytes=16 * 1024 * 1024),
    )(message)
    return result[None, None]


def solution(mesh):
    def program(state, mean_flow, les_owner, ac_owner, les_nbr, ac_nbr, coupling):
        plan = Plan(mesh.shape["block"], mesh.shape["section"], state.shape[2], state.shape[3])
        return jax.shard_map(
            functools.partial(on_device, plan),
            mesh=mesh,
            in_specs=(
                P("section", "block", None, None, None),
                P("block", None, None, None),
                P(),
                P(),
                P(),
                P(),
                P(),
            ),
            out_specs=P("section", "block", None, None, None),
            check_vma=False,
        )(state, mean_flow, les_owner, ac_owner, les_nbr, ac_nbr, coupling)

    return program
```

```python
import functools

import jax
import jax.numpy as jnp
from jax import lax
from jax.experimental import pallas as pl
from jax.experimental.pallas import tpu as pltpu
from jax.sharding import PartitionSpec as P


STEPS = 2

GAMMA_LESS = 0.4
DT_LES = 0.2
DT_AC = 0.3
VISCOSITY = 0.05
FEEDBACK_GAIN = 0.5

WIRE = jnp.int16
SCALE_IN = 16384.0
SCALE_MID = 8192.0
SCALE_OUT = 4096.0
OFFSETS = ((1.25, 0.0, 0.0, 0.0, 2.6), (0.0, 0.0, 0.0, 0.0, 0.0))
MEAN_OFFSETS = (1.0, 0.0, 0.0, 0.0, 1.0)
PAIRS = ((0, 1), (2, 3), (4, 4))

LANES = 128
FACES = 6
COLUMNS = FACES + 1


class Plan:
    def __init__(self, blocks, sections, num_vars, side):
        self.blocks = blocks
        self.devices = blocks * sections
        self.vars = num_vars
        self.side = side
        self.layers_z = blocks // 16
        self.ny = side * side // LANES
        self.nx = self.devices // self.ny
        self.xs = side // self.nx
        self.half = self.xs // sections
        self.core_rows = num_vars * self.xs
        self.y_base = self.core_rows
        self.mean_base = self.y_base + len(PAIRS) * self.xs
        self.x_base = self.mean_base + num_vars * self.half
        self.rows = -(-(self.x_base + 2 * num_vars) // 16) * 16
        assert self.nx > 1 and sections == 2 and LANES == 4 * side and 2 * self.half * self.nx == side

    def piece(self, device):
        section, block = device // self.blocks, device % self.blocks
        low, mid, high = block % 2, block // 2 % 2, block // 4
        ring = section if low == 0 else 3 - section
        depth = high % 4
        return ring + 4 * (high // 4), depth if mid == 0 else 7 - depth

    def own_piece(self, section, block):
        low, mid, high = block % 2, block // 2 % 2, block // 4
        ring = jnp.where(low == 0, section, 3 - section)
        depth = high % 4
        return ring + 4 * (high // 4), jnp.where(mid == 0, depth, 7 - depth)

    def permutation(self, step_x, step_y):
        at = {self.piece(d): d for d in range(self.devices)}
        assert len(at) == self.devices
        pairs = []
        for device in range(self.devices):
            px, py = self.piece(device)
            pairs.append((device, at[((px + step_x) % self.nx, (py + step_y) % self.ny)]))
        return pairs


def to_wire(scaled):
    return lax.round(scaled, lax.RoundingMethod.TO_NEAREST_EVEN).astype(jnp.int32).astype(WIRE)


def from_wire(sent):
    return sent.astype(jnp.int32).astype(jnp.float32)


def roll_lanes(tile, shift):
    shift = shift % LANES
    return pltpu.roll(tile, shift, 1) if shift else tile


def roll_rows(tile, shift):
    rows = tile.shape[0]
    shift = shift % rows
    if rows % 8 == 0:
        return pltpu.roll(tile, shift, 0)
    return jnp.concatenate([tile[rows - shift :], tile[: rows - shift]], axis=0)


def lane_index(rows):
    return lax.broadcasted_iota(jnp.int32, (rows, LANES), 1)


def pack_kernel(
    plan, state_hbm, mean_hbm, *refs
):
    lookups_hbm, (message, table), rest = refs[:5], refs[5:7], refs[7:]
    lookups, rest = rest[:5], rest[5:]
    state, mean, filled, *found = rest[:-3]
    small_sem, state_sem, mean_sem = rest[-3:]
    small = [
        pltpu.make_async_copy(source, target, small_sem.at[i])
        for i, (source, target) in enumerate(zip(lookups_hbm, lookups))
    ]
    for copy in small:
        copy.start()
    large = []
    for v in range(plan.vars):
        large.append(pltpu.make_async_copy(state_hbm.at[v], state.at[v], state_sem.at[v]))
        large.append(pltpu.make_async_copy(mean_hbm.at[v], mean.at[v], mean_sem.at[v]))
    for copy in large:
        copy.start()
    section = lax.axis_index("section")
    px, py = plan.own_piece(section, lax.axis_index("block"))
    for copy in small:
        copy.wait()
    invert(plan, lookups, *found)

    xs, side, half = plan.xs, plan.side, plan.half
    width = side * side
    lane = lane_index(xs)
    outer = (lane < side) | (lane >= LANES - side)
    pieces = []
    for device in range(plan.devices):
        tx, ty = plan.piece(device)
        pieces.append((device, tx * xs, ty * LANES))
    whole = xs % 8 == 0
    gathered = plan.mean_base if whole else 0

    def put(device, start, tile):
        if whole:
            message[device, start : start + xs, :] = to_wire(tile)
        else:
            filled[device, start : start + xs, :] = tile

    used = plan.x_base + 2 * plan.vars
    for v in range(plan.vars):
        large[2 * v].wait()
        for slot in range(v * plan.blocks // plan.vars, (v + 1) * plan.blocks // plan.vars):
            look_up(plan, px, py, table, lookups, *found, slot)
        offset = jnp.where(section == 0, OFFSETS[0][v], OFFSETS[1][v])
        state[v] = (state[v] - offset) * SCALE_IN
        for device, x0, l0 in pieces:
            here = slice(l0, l0 + LANES)
            put(device, v * xs, state[v, x0 : x0 + xs, here])
            filled[device, plan.x_base + v, :] = state[v, (x0 - 1) % side, here]
            filled[device, plan.x_base + plan.vars + v, :] = state[v, (x0 + xs) % side, here]
        if v % 2 == 1 or v == plan.vars - 1:
            i, (a, b) = v // 2, PAIRS[v // 2]
            for device, x0, l0 in pieces:
                before = (l0 - LANES) % width
                after = (l0 + LANES) % width
                edge = [
                    jnp.where(
                        lane >= LANES - side,
                        state[u, x0 : x0 + xs, before : before + LANES],
                        state[u, x0 : x0 + xs, after : after + LANES],
                    )
                    for u in ((a, b) if a != b else (a,))
                ]
                tile = edge[0]
                if a != b:
                    tile = jnp.where(outer, edge[0], roll_lanes(edge[1], LANES // 2))
                put(device, plan.y_base + i * xs, tile)
        large[2 * v + 1].wait()
        for device, x0, l0 in pieces:
            here = slice(l0, l0 + LANES)
            first, second = mean[v, x0 : x0 + half, here], mean[v, x0 + half : x0 + xs, here]
            piece = jnp.where(section == 0, first, second)
            base = plan.mean_base + v * half
            filled[device, base : base + half, :] = (piece - MEAN_OFFSETS[v]) * SCALE_IN
    for device, _, _ in pieces:
        if used < plan.rows:
            filled[device, used:, :] = jnp.zeros((plan.rows - used, LANES), jnp.float32)
        message[device, gathered:, :] = to_wire(filled[device, gathered:, :])


def invert(plan, lookups, les_inv, ac_inv, pair_inv, les_slots, ac_slots):
    les_owner, ac_owner, _, _, coupling = lookups
    les_slots[0] = -1
    ac_slots[0] = -1
    for i in range(plan.blocks):
        les, ac = les_owner[i], ac_owner[i]
        les_inv[les] = i
        ac_inv[ac] = i
        les_slots[i + 1] = les
        ac_slots[i + 1] = ac
        pair_inv[coupling[i]] = i


def look_up(plan, px, py, table, lookups, les_inv, ac_inv, pair_inv, les_slots, ac_slots, slot):
    les_owner, ac_owner, les_nbr, ac_nbr, coupling = lookups
    les_block = les_inv[slot]
    ac_block = ac_inv[slot]
    for kind, (block, nbr, slots) in enumerate(
        ((les_block, les_nbr, les_slots), (ac_block, ac_nbr, ac_slots))
    ):

        def write(face, value):
            table[(kind * COLUMNS + face) * plan.blocks + slot] = value

        for axis, (at, count) in enumerate(((px, plan.nx), (py, plan.ny))):
            low, high = at == 0, at == count - 1
            source = slots[nbr[jnp.where(low, 2 * axis, 2 * axis + 1), block] + 1]
            write(2 * axis, jnp.where(low, source, slot))
            write(2 * axis + 1, jnp.where(high, source, slot))
        if plan.layers_z > 1:
            for face in (4, 5):
                write(face, slots[nbr[face, block] + 1])
    table[FACES * plan.blocks + slot] = ac_owner[pair_inv[les_block]]
    table[(COLUMNS + FACES) * plan.blocks + slot] = les_owner[coupling[ac_block]]


def sides_xy(plan, table, kind, slot, own, x_halo, y_halo):
    xs, side = plan.xs, plan.side
    lane = lane_index(xs)
    row = lax.broadcasted_iota(jnp.int32, (xs, LANES), 0)
    found = [table[(kind * COLUMNS + face) * plan.blocks + slot] for face in range(4)]
    inside = [f >= 0 for f in found]
    found = [jnp.maximum(f, 0) for f in found]
    shifted = [[] for _ in range(4)]
    for v, tile in enumerate(own):
        low = jnp.where(inside[0], x_halo(kind, found[0], v, 0), tile)
        high = jnp.where(inside[1], x_halo(kind, found[1], v, 1), tile)
        shifted[0].append(jnp.where(row == 0, low, roll_rows(tile, 1)))
        shifted[1].append(jnp.where(row == xs - 1, high, roll_rows(tile, -1)))
        low = roll_lanes(jnp.where(lane >= LANES - side, y_halo(kind, found[2], v, 0), tile), side)
        high = roll_lanes(jnp.where(lane < side, y_halo(kind, found[3], v, 1), tile), -side)
        shifted[2].append(jnp.where((lane < side) & ~inside[2], tile, low))
        shifted[3].append(jnp.where((lane >= LANES - side) & ~inside[3], tile, high))
    return shifted


def sides_z(plan, table, kind, slot, own, core):
    side = plan.side
    depth = lane_index(plan.xs) % side
    shifted = [[], []]
    if plan.layers_z > 1:
        found = [table[(kind * COLUMNS + face) * plan.blocks + slot] for face in (4, 5)]
        inside = [f >= 0 for f in found]
        found = [jnp.maximum(f, 0) for f in found]
    for v, tile in enumerate(own):
        low, high = tile, tile
        if plan.layers_z > 1:
            low = jnp.where(inside[0], roll_lanes(core(kind, found[0], v), 1 - side), tile)
            high = jnp.where(inside[1], roll_lanes(core(kind, found[1], v), side - 1), tile)
        shifted[0].append(jnp.where(depth == 0, low, roll_lanes(tile, 1)))
        shifted[1].append(jnp.where(depth == side - 1, high, roll_lanes(tile, -1)))
    return shifted


def ends(plan):
    lane = lane_index(plan.xs)
    row = lax.broadcasted_iota(jnp.int32, (plan.xs, LANES), 0)
    return (
        (row == 0, row == plan.xs - 1),
        (lane < plan.side, lane >= LANES - plan.side),
    )


def sides_inner(plan, own):
    (x_low, x_high), (y_low, y_high) = ends(plan)
    side = plan.side
    return [
        ([roll_rows(t, 1) for t in own], x_low, [roll_rows(t, -1) for t in own], x_high),
        ([roll_lanes(t, side) for t in own], y_low, [roll_lanes(t, -side) for t in own], y_high),
    ]


def states_outer(plan, table, kind, slot, own, x_halo, y_halo):
    (x_low, _), (y_low, _) = ends(plan)
    found = [table[(kind * COLUMNS + face) * plan.blocks + slot] for face in range(4)]
    inside = [f >= 0 for f in found]
    found = [jnp.maximum(f, 0) for f in found]
    along_x, along_y = [], []
    for v, tile in enumerate(own):
        low = jnp.where(inside[0], x_halo(kind, found[0], v, 0), tile)
        high = jnp.where(inside[1], x_halo(kind, found[1], v, 1), tile)
        along_x.append(jnp.where(x_low, low, high))
        low = jnp.where(inside[2], y_halo(kind, found[2], v, 0), tile)
        high = jnp.where(inside[3], y_halo(kind, found[3], v, 1), tile)
        along_y.append(jnp.where(y_low, low, high))
    return along_x, along_y


def at_ends(plan, low_value, high_value):
    return [
        jnp.where(low, low_value, jnp.where(high, high_value, 0.0)).astype(jnp.float32)
        for low, high in ends(plan)
    ]


def primitives(conserved):
    density, energy = conserved[0], conserved[4]
    momentum = conserved[1:4]
    inverse = 1.0 / density
    velocity = [m * inverse for m in momentum]
    kinetic = momentum[0] * velocity[0] + momentum[1] * velocity[1] + momentum[2] * velocity[2]
    return momentum, energy, velocity, GAMMA_LESS * (energy - 0.5 * kinetic)


def flux_along(conserved, axis):
    momentum, energy, velocity, pressure = primitives(conserved)
    normal = velocity[axis]
    flux = [momentum[axis]]
    for component in range(3):
        entry = momentum[component] * normal
        flux.append(entry + pressure if component == axis else entry)
    flux.append((energy + pressure) * normal)
    return flux, velocity


def cross(a, b):
    return [
        a[1] * b[2] - a[2] * b[1],
        a[2] * b[0] - a[0] * b[2],
        a[0] * b[1] - a[1] * b[0],
    ]


def as_bf16(tile):
    return tile.astype(jnp.bfloat16).astype(jnp.float32)


def plus(total, term):
    return term if total is None else total + term


def les_axes(plan, total, axes, pairs):
    nearby, outflow = [None] * plan.vars, [None] * plan.vars
    gradient = []
    for axis, (low, high) in zip(axes, pairs):
        flux_low, speed_low = flux_along(low, axis)
        flux_high, speed_high = flux_along(high, axis)
        for v in range(plan.vars):
            nearby[v] = plus(nearby[v], low[v] + high[v])
            outflow[v] = plus(outflow[v], flux_high[v] - flux_low[v])
        gradient.append([h - w for h, w in zip(speed_high, speed_low)])
    near, out = 0.5 * DT_LES * VISCOSITY, 0.25 * DT_LES
    return [t + (near * n - out * o) for t, n, o in zip(total, nearby, outflow)], gradient


def les_z(plan, table, slot, core, unit):
    own = [core(0, slot, v) for v in range(plan.vars)]
    total = [(0.5 - 3.0 * DT_LES * VISCOSITY) * g for g in own]
    total, gradient = les_axes(plan, total, (2,), [sides_z(plan, table, 0, slot, own, core)])
    partner = table[FACES * plan.blocks + slot]
    for j in range(3):
        back = as_bf16(core(1, partner, 1 + j))
        total[1 + j] = total[1 + j] + (0.5 * DT_LES * FEEDBACK_GAIN) * back
    inverse = unit / own[0]
    return total + gradient[0][:2] + [m * inverse for m in own[1:4]]


def les_xy(plan, part, shifted):
    count = plan.vars
    pairs = [shifted[0:2], shifted[2:4]]
    total, (along_x, along_y) = les_axes(plan, part[:count], (0, 1), pairs)
    along_z, velocity = part[count : count + 2], part[count + 2 :]
    vorticity = [along_y[2] - along_z[1], along_z[0] - along_x[2], along_x[1] - along_y[0]]
    return total, [as_bf16(t) for t in cross(vorticity, velocity)]


def les_inner(plan, table, slot, core, unit):
    own = [core(0, slot, v) for v in range(plan.vars)]
    part = les_z(plan, table, slot, core, unit)
    total, velocity = part[: plan.vars], part[plan.vars + 2 :]
    along_z = part[plan.vars : plan.vars + 2]
    near, out = 0.5 * DT_LES * VISCOSITY, 0.25 * DT_LES
    gradient = []
    for axis, (low, low_end, high, high_end) in enumerate(sides_inner(plan, own)):
        flux_low, speed_low = flux_along(low, axis)
        flux_high, speed_high = flux_along(high, axis)
        for v in range(plan.vars):
            from_low = jnp.where(low_end, 0.0, near * low[v] + out * flux_low[v])
            from_high = jnp.where(high_end, 0.0, near * high[v] - out * flux_high[v])
            total[v] = total[v] + (from_low + from_high)
        gradient.append(
            [
                jnp.where(high_end, 0.0, h) - jnp.where(low_end, 0.0, w)
                for h, w in zip(speed_high, speed_low)
            ]
        )
    along_x, along_y = gradient
    vorticity = [along_y[2] - along_z[1], along_z[0] - along_x[2], along_x[1] - along_y[0]]
    return total + vorticity + velocity


def les_outer(plan, part, states):
    count = plan.vars
    total, vorticity, velocity = part[:count], part[count : count + 3], part[count + 3 :]
    near = at_ends(plan, 0.5 * DT_LES * VISCOSITY, 0.5 * DT_LES * VISCOSITY)
    out = at_ends(plan, 0.25 * DT_LES, -0.25 * DT_LES)
    sign = at_ends(plan, -1.0, 1.0)
    gradient = []
    for axis, state in enumerate(states):
        flux, speed = flux_along(state, axis)
        total = [t + (near[axis] * g + out[axis] * f) for t, g, f in zip(total, state, flux)]
        gradient.append([sign[axis] * u for u in speed])
    along_x, along_y = gradient
    vorticity = [
        vorticity[0] + along_y[2],
        vorticity[1] - along_x[2],
        vorticity[2] + (along_x[1] - along_y[0]),
    ]
    return total, [as_bf16(t) for t in cross(vorticity, velocity)]


def ac_axes(plan, total, axes, pairs, mean, source):
    slope = [[h - w for h, w in zip(high, low)] for low, high in pairs]
    return ac_slopes(plan, total, axes, slope, mean, source)


def ac_slopes(plan, total, axes, slope, mean, source):
    change = [None] * plan.vars
    divergence = None
    for axis, s in zip(axes, slope):
        change = [plus(c, mean[1 + axis] * t) for c, t in zip(change, s)]
        divergence = plus(divergence, s[1 + axis])
    inverse = 1.0 / mean[0]
    for axis, s in zip(axes, slope):
        change[1 + axis] = change[1 + axis] + s[4] * inverse
    if source is not None:
        change[1:4] = [c + t for c, t in zip(change[1:4], source)]
    change[0] = change[0] + mean[0] * divergence
    change[4] = change[4] + 1.4 * mean[4] * divergence
    return [t - (0.25 * DT_AC) * c for t, c in zip(total, change)]


def ac_z(plan, table, slot, core, mean):
    own = [core(1, slot, v) for v in range(plan.vars)]
    pair = sides_z(plan, table, 1, slot, own, core)
    return ac_axes(plan, [0.5 * g for g in own], (2,), [pair], mean(slot), None)


def ac_inner(plan, table, slot, core, mean):
    own = [core(1, slot, v) for v in range(plan.vars)]
    slope = []
    for low, low_end, high, high_end in sides_inner(plan, own):
        slope.append(
            [
                jnp.where(high_end, 0.0, h) - jnp.where(low_end, 0.0, w)
                for h, w in zip(high, low)
            ]
        )
    low, high = sides_z(plan, table, 1, slot, own, core)
    slope.append([h - w for h, w in zip(high, low)])
    return ac_slopes(plan, [0.5 * g for g in own], (0, 1, 2), slope, mean(slot), None)


def ac_outer(plan, part, states, mean, source):
    sign = at_ends(plan, -1.0, 1.0)
    slope = [[sign[axis] * g for g in state] for axis, state in enumerate(states)]
    return ac_slopes(plan, part, (0, 1), slope, mean, source)


def advance(plan, table, core, lamb, les, ac, store):
    xs = plan.xs

    def les_quad(quad, carry):
        results = []
        for r in range(4):
            slot = quad * 4 + r
            own = [core(0, slot, v) for v in range(plan.vars)]
            total, vector = les(slot, own)
            for j in range(3):
                lamb[slot, j * xs : (j + 1) * xs, :] = vector[j]
            results.append(total)
        store(0, quad, results)
        return carry

    def ac_quad(quad, carry):
        results = []
        for r in range(4):
            slot = quad * 4 + r
            own = [core(1, slot, v) for v in range(plan.vars)]
            partner = table[(COLUMNS + FACES) * plan.blocks + slot]
            source = [lamb[partner, j * xs : (j + 1) * xs, :] for j in range(3)]
            results.append(ac(slot, own, source))
        store(1, quad, results)
        return carry

    lax.fori_loop(0, plan.blocks // 4, les_quad, 0)
    lax.fori_loop(0, plan.blocks // 4, ac_quad, 0)


def tile_rows(plan, v):
    return slice(v * plan.xs, (v + 1) * plan.xs)


def first_kernel(
    plan, table, message,
    after, mean_out, x_up, x_down, y_up, y_down,
    arrived, origin, lamb, x_up_raw, x_down_raw, y_up_raw, y_down_raw,
):
    xs, side, count, blocks, half = plan.xs, plan.side, plan.vars, plan.blocks, plan.half
    lane = lane_index(xs)
    outer = (lane < side) | (lane >= LANES - side)

    for kind in range(2):
        origin[kind] = jnp.zeros((plan.rows, LANES), jnp.float32)
        for v, offset in enumerate(MEAN_OFFSETS):
            base = plan.mean_base + v * half
            origin[kind, base : base + half, :] = jnp.full((half, LANES), offset * SCALE_IN, jnp.float32)
        for v, offset in enumerate(OFFSETS[kind]):
            if offset == 0.0:
                continue
            level = jnp.full((xs, LANES), offset * SCALE_IN, jnp.float32)
            origin[kind, tile_rows(plan, v), :] = level
            for end in range(2):
                origin[kind, plan.x_base + end * count + v, :] = level[0]
            base = plan.y_base + (v // 2) * xs
            origin[kind, base : base + xs, :] = jnp.where(outer, level, 0.0)

    def read(slot, carry):
        for kind in range(2):
            arrived[kind * blocks + slot] = from_wire(message[kind * blocks + slot]) + origin[kind]
        return carry

    lax.fori_loop(0, blocks, read, 0, unroll=2)

    def read_mean(slot, carry):
        for v in range(count):
            base = plan.mean_base + v * half
            for part in range(plan.devices // blocks):
                rows = arrived[part * blocks + slot, base : base + half, :]
                start = v * xs + part * half
                mean_out[slot, start : start + half, :] = rows * (1.0 / SCALE_IN)
        return carry

    lax.fori_loop(0, blocks, read_mean, 0, unroll=4)

    def core(kind, slot, v):
        return arrived[kind * blocks + slot, tile_rows(plan, v), :]

    def x_halo(kind, slot, v, end):
        at = plan.x_base + end * count + v
        return arrived[kind * blocks + slot, pl.ds(at, xs, stride=0), :]

    def y_halo(kind, slot, v, end):
        base = plan.y_base + (v // 2) * xs
        tile = arrived[kind * blocks + slot, base : base + xs, :]
        return roll_lanes(tile, LANES // 2) if v % 2 == 1 else tile

    def mean(slot):
        return [mean_out[slot, tile_rows(plan, v), :] for v in range(count)]

    def in_quarters(tiles, first):
        packed = None
        for quarter, tile in enumerate(tiles):
            moved = roll_lanes(tile, side * (quarter - first))
            packed = moved if packed is None else jnp.where(lane >= side * quarter, moved, packed)
        return packed

    def store(kind, quad, results):
        rest = []
        for r, tiles in enumerate(results):
            m = kind * blocks + quad * 4 + r
            coded = []
            for v, tile in enumerate(tiles):
                after[m, tile_rows(plan, v), :] = tile
                offset = OFFSETS[kind][v] * SCALE_MID
                coded.append(tile if offset == 0.0 else tile - offset)
                x_up_raw[pl.ds(m * count + v, 1), :] = coded[v][xs - 1 : xs]
                x_down_raw[pl.ds(m * count + v, 1), :] = coded[v][0:1]
            rest.append(coded[4])
            where = pl.ds(pl.multiple_of(m * xs, xs), xs)
            y_up_raw[where, :] = in_quarters(coded[:4], 3)
            y_down_raw[where, :] = in_quarters(coded[:4], 0)
        start = (plan.devices + kind * (blocks // 4) + quad) * xs
        where = pl.ds(pl.multiple_of(start, xs), xs)
        y_up_raw[where, :] = in_quarters(rest, 3)
        y_down_raw[where, :] = in_quarters(rest, 0)

    def les(slot, own):
        shifted = sides_xy(plan, table, 0, slot, own, x_halo, y_halo)
        return les_xy(plan, les_z(plan, table, slot, core, SCALE_IN), shifted)

    def ac(slot, own, source):
        shifted = sides_xy(plan, table, 1, slot, own, x_halo, y_halo)
        pairs = [shifted[0:2], shifted[2:4]]
        part = ac_z(plan, table, slot, core, mean)
        return ac_axes(plan, part, (0, 1), pairs, mean(slot), source)

    advance(plan, table, core, lamb, les, ac, store)
    for raw, out in (
        (x_up_raw, x_up), (x_down_raw, x_down), (y_up_raw, y_up), (y_down_raw, y_down),
    ):
        out[...] = to_wire(raw[...])


def middle_les_kernel(plan, table, before, out):
    def core(kind, slot, v):
        return before[kind * plan.blocks + slot, tile_rows(plan, v), :]

    def body(slot, carry):
        for i, tile in enumerate(les_inner(plan, table, slot, core, SCALE_MID)):
            out[slot, tile_rows(plan, i), :] = tile
        return carry

    lax.fori_loop(0, plan.blocks, body, 0, unroll=4)


def middle_ac_kernel(plan, table, before, mean_in, out):
    def core(kind, slot, v):
        return before[kind * plan.blocks + slot, tile_rows(plan, v), :]

    def mean(slot):
        return [mean_in[slot, tile_rows(plan, v), :] for v in range(plan.vars)]

    def body(slot, carry):
        for v, tile in enumerate(ac_inner(plan, table, slot, core, mean)):
            out[slot, tile_rows(plan, v), :] = tile
        return carry

    lax.fori_loop(0, plan.blocks, body, 0, unroll=4)


def last_kernel(
    plan, table, before, mean_in, les_in, ac_in, x_low, x_high, y_low, y_high,
    message, lamb, x_low_raw, x_high_raw, y_low_raw, y_high_raw, coded,
):
    xs, side, count, blocks = plan.xs, plan.side, plan.vars, plan.blocks
    for raw, sent in (
        (x_low_raw, x_low), (x_high_raw, x_high), (y_low_raw, y_low), (y_high_raw, y_high),
    ):
        raw[...] = from_wire(sent[...])

    def shift_back(tile, kind, v):
        offset = OFFSETS[kind][v] * SCALE_MID
        return tile if offset == 0.0 else tile + offset

    def core(kind, slot, v):
        return before[kind * blocks + slot, tile_rows(plan, v), :]

    def x_halo(kind, slot, v, end):
        raw = x_high_raw if end else x_low_raw
        at = (kind * blocks + slot) * count + v
        return shift_back(raw[pl.ds(at, xs, stride=0), :], kind, v)

    def y_halo(kind, slot, v, end):
        raw = y_high_raw if end else y_low_raw
        m = kind * blocks + slot
        target = 3 * side if end else 0
        if v < 4:
            tile = raw[pl.ds(pl.multiple_of(m * xs, xs), xs), :]
            tile = roll_lanes(tile, target - side * v)
        else:
            rest = plan.devices * xs + (m >> 2) * xs
            tile = raw[pl.ds(pl.multiple_of(rest, xs), xs), :]
            tile = pltpu.roll(tile, (target + LANES - side * (m & 3)) & (LANES - 1), 1)
        return shift_back(tile, kind, v)

    def mean(slot):
        return [mean_in[slot, tile_rows(plan, v), :] for v in range(count)]

    def store(kind, quad, results):
        for r, tiles in enumerate(results):
            for v, tile in enumerate(tiles):
                offset = OFFSETS[kind][v] * SCALE_OUT
                tile = tile if offset == 0.0 else tile - offset
                coded[kind * blocks + quad * 4 + r, tile_rows(plan, v), :] = tile

    def les(slot, own):
        part = [les_in[slot, tile_rows(plan, i), :] for i in range(count + 6)]
        return les_outer(plan, part, states_outer(plan, table, 0, slot, own, x_halo, y_halo))

    def ac(slot, own, source):
        part = [ac_in[slot, tile_rows(plan, v), :] for v in range(count)]
        states = states_outer(plan, table, 1, slot, own, x_halo, y_halo)
        return ac_outer(plan, part, states, mean(slot), source)

    advance(plan, table, core, lamb, les, ac, store)

    def write(m, carry):
        message[m] = to_wire(coded[m])
        return carry

    lax.fori_loop(0, plan.devices, write, 0, unroll=4)


def unpack_kernel(plan, message, out):
    section = lax.axis_index("section")
    xs = plan.xs
    for device in range(plan.devices):
        tx, ty = plan.piece(device)
        values = from_wire(message[device]) * (1.0 / SCALE_OUT)
        for v in range(plan.vars):
            offset = jnp.where(section == 0, OFFSETS[0][v], OFFSETS[1][v])
            out[v, tx * xs : (tx + 1) * xs, ty * LANES : (ty + 1) * LANES] = (
                values[v * xs : (v + 1) * xs] + offset
            )


def vmem(count):
    return [pl.BlockSpec(memory_space=pltpu.VMEM)] * count


def smem(count):
    return [pl.BlockSpec(memory_space=pltpu.SMEM)] * count


def on_device(plan, state, mean_flow, les_owner, ac_owner, les_nbr, ac_nbr, coupling):
    axes = ("section", "block")
    devices, blocks, count, xs = plan.devices, plan.blocks, plan.vars, plan.xs
    f32 = jnp.float32

    def array(dtype, *shape):
        return jax.ShapeDtypeStruct(shape, dtype)

    far = [
        pltpu.with_memory_space_constraint(a, pltpu.HBM)
        for a in (state[0, 0], mean_flow[0], les_owner, ac_owner, les_nbr.T, ac_nbr.T, coupling)
    ]
    volume = pltpu.VMEM((count, plan.side, plan.side * plan.side), f32)
    lookups = [pltpu.SMEM(a.shape, jnp.int32) for a in far[2:]]
    message, table = pl.pallas_call(
        functools.partial(pack_kernel, plan),
        out_shape=(
            array(WIRE, devices, plan.rows, LANES),
            pltpu.SMEM((2 * COLUMNS * blocks,), jnp.int32),
        ),
        in_specs=[pl.BlockSpec(memory_space=pltpu.HBM)] * len(far),
        out_specs=tuple(vmem(1) + smem(1)),
        scratch_shapes=lookups
        + [volume, volume, pltpu.VMEM((devices, plan.rows, LANES), f32)]
        + [pltpu.SMEM((blocks,), jnp.int32)] * 3
        + [pltpu.SMEM((blocks + 1,), jnp.int32)] * 2
        + [pltpu.SemaphoreType.DMA((n,)) for n in (len(lookups), count, count)],
        name="pack",
        compiler_params=pltpu.CompilerParams(vmem_limit_bytes=16 * 1024 * 1024),
    )(*far)
    message = lax.all_to_all(message, axes, split_axis=0, concat_axis=0, tiled=True)

    x_rows = devices * count
    y_rows = devices * xs + devices // 4 * xs
    halo_shapes = [(x_rows, LANES)] * 2 + [(y_rows, LANES)] * 2
    halo_scratch = [pltpu.VMEM(shape, f32) for shape in halo_shapes]
    lamb_scratch = pltpu.VMEM((blocks, 3 * xs, LANES), f32)
    after, mean, *halos = pl.pallas_call(
        functools.partial(first_kernel, plan),
        out_shape=(
            array(f32, devices, plan.core_rows, LANES),
            array(f32, blocks, plan.core_rows, LANES),
            *(array(WIRE, *shape) for shape in halo_shapes),
        ),
        in_specs=smem(1) + vmem(1),
        out_specs=tuple(vmem(6)),
        scratch_shapes=[
            pltpu.VMEM((devices, plan.rows, LANES), f32),
            pltpu.VMEM((2, plan.rows, LANES), f32),
            lamb_scratch,
        ]
        + halo_scratch,
        name="first_step",
        compiler_params=pltpu.CompilerParams(vmem_limit_bytes=16 * 1024 * 1024),
    )(table, message)
    moves = [plan.permutation(*step) for step in ((1, 0), (-1, 0), (0, 1), (0, -1))]
    halos = [lax.ppermute(halo, axes, move) for halo, move in zip(halos, moves)]

    les_part = pl.pallas_call(
        functools.partial(middle_les_kernel, plan),
        out_shape=array(f32, blocks, (count + 6) * xs, LANES),
        in_specs=smem(1) + vmem(1),
        out_specs=vmem(1)[0],
        name="middle_les",
        compiler_params=pltpu.CompilerParams(vmem_limit_bytes=16 * 1024 * 1024),
    )(table, after)
    ac_part = pl.pallas_call(
        functools.partial(middle_ac_kernel, plan),
        out_shape=array(f32, blocks, plan.core_rows, LANES),
        in_specs=smem(1) + vmem(2),
        out_specs=vmem(1)[0],
        name="middle_ac",
        compiler_params=pltpu.CompilerParams(vmem_limit_bytes=16 * 1024 * 1024),
    )(table, after, mean)
    message = pl.pallas_call(
        functools.partial(last_kernel, plan),
        out_shape=array(WIRE, devices, plan.core_rows, LANES),
        in_specs=smem(1) + vmem(8),
        out_specs=vmem(1)[0],
        scratch_shapes=[lamb_scratch]
        + halo_scratch
        + [pltpu.VMEM((devices, plan.core_rows, LANES), f32)],
        name="last_step",
        compiler_params=pltpu.CompilerParams(vmem_limit_bytes=16 * 1024 * 1024),
    )(table, after, mean, les_part, ac_part, *halos)
    message = lax.all_to_all(message, axes, split_axis=0, concat_axis=0, tiled=True)

    result = pl.pallas_call(
        functools.partial(unpack_kernel, plan),
        out_shape=array(f32, *state.shape[2:]),
        in_specs=vmem(1),
        out_specs=vmem(1)[0],
        name="unpack",
        compiler_params=pltpu.CompilerParams(vmem_limit_bytes=16 * 1024 * 1024),
    )(message)
    return result[None, None]


def solution(mesh):
    def program(state, mean_flow, les_owner, ac_owner, les_nbr, ac_nbr, coupling):
        plan = Plan(mesh.shape["block"], mesh.shape["section"], state.shape[2], state.shape[3])
        return jax.shard_map(
            functools.partial(on_device, plan),
            mesh=mesh,
            in_specs=(
                P("section", "block", None, None, None),
                P("block", None, None, None),
                P(),
                P(),
                P(),
                P(),
                P(),
            ),
            out_specs=P("section", "block", None, None, None),
            check_vma=False,
        )(state, mean_flow, les_owner, ac_owner, les_nbr, ac_nbr, coupling)

    return program
```
